32 devices in a mesh: dp: 4 (over y, x), graph: 8 (over z, core).
Axes of the slice: x: 2, y: 2, z: 4, core: 2. Of those that a mesh axis runs over, the one named last changes fastest.
Arguments:
- messages: bfloat16 [4, 8192, 512], P('dp', 'graph'), may hold values from -6 to 6
- cotangent: bfloat16 [4, 8192, 512], P('dp', 'graph'), may hold values from -6 to 6
- triplet_basis: bfloat16 [4, 8192, 3584], P('dp', 'graph'), may hold values from -6 to 6
- w_edge: bfloat16 [512, 512], replicated, may hold values from -0.25 to 0.25
- w_down: bfloat16 [512, 64], replicated, may hold values from -0.25 to 0.25
- w_bil: bfloat16 [112, 4096], replicated, may hold values from -0.01171875 to 0.01171875
- w_up: bfloat16 [2, 64, 512], replicated, may hold values from -0.75 to 0.75
- trip_src: int32 [4, 8192, 32], P('dp', 'graph'), may hold values from -1 to 2047, as said below
- send_rows: int32 [4, 32, 256], P('dp', 'graph'), may hold values from 0 to 1023, as said below
- send_count: int32 [4, 32], P('dp', 'graph'), may hold values from 1 to 256, as said below
- rev_src: int32 [4, 8192], P('dp', 'graph'), may hold values from -1 to 2047, as said below
- edge_count: int32 [4, 8], P('dp', 'graph'), may hold values from 614 to 1024, as said below
Outputs:
- grad_messages: bfloat16 [4, 8192, 512], P('dp', 'graph')
- grad_w_edge: float32 [512, 512], P('graph')
- grad_w_down: float32 [512, 64], P('graph')
- grad_w_bil: float32 [112, 4096], P(None, 'graph')
- grad_w_up: float32 [2, 64, 512], P(None, None, 'graph')
The draws below stay inside these ranges and needn't reach their ends.
Inputs may be any that keep to these rules, and one draw needn't show every extreme that they name: `trip_src`: an entry below 1024 is a live edge of the same device; an entry 1024 + o * 256 + c names row c, below its count, of send list o of the device off(o) positions lower along graph (cyclically). Slots k at or beyond an edge's triplet count, and all slots of empty edges, are -1. `send_rows`: send list o of a device goes to the device off(o) positions higher along graph, cyclically. Its entries are distinct live rows; entries at or beyond the list's count are padding. `send_count`: in each slab some list holds exactly 256 rows. `rev_src`: every live edge has one reverse edge, on its own device or within 2 devices; if edge e reads row r as its reverse, the edge behind r reads e back. Empty slots hold -1. `edge_count`: in each slab some device is full.
All inputs are finite; a program needn't handle non-finite values.
Results may differ from the reference program's by a relative error of at most 0.023.
Values may be sent and summed in bfloat16 or wider, within the bound.
No kernel may reach another device: no remote copies, remote signals or barrier semaphores. Data moves between devices by JAX's collectives and lax.ppermute only.
A program may use at most 192 MiB of HBM per device.

```python
import jax
import jax.numpy as jnp
from jax import lax

D = 512
TW = 64
NB = 112
E_DEV = 1024
K = 32
REACH = 2
CAP = 256
POOL = 2048
EDGES = 8192
SLABS = 4
N_GRAPH = 8


def offsets_drawn(count):
    return [(which // 2 + 1) * (1 - 2 * (which % 2)) for which in range(count)]


def build_slab(key):
    devices = N_GRAPH
    edges = E_DEV
    list_count = 2 * REACH
    shifts = offsets_drawn(list_count)
    keys = jax.random.split(key, 12)
    pair_half = 2 * jax.random.randint(keys[0], (devices, REACH), CAP // 8, CAP // 4 + 1)
    columns = []
    for which in range(list_count):
        reach_index = abs(shifts[which]) - 1
        if shifts[which] > 0:
            columns.append(pair_half[:, reach_index])
        else:
            columns.append(jnp.roll(pair_half[:, reach_index], -shifts[which], axis=0))
    pair_count = jnp.stack(columns, axis=1)
    block_end = jnp.cumsum(pair_count, axis=1)
    block_start = block_end - pair_count
    remote = block_end[:, -1]
    halves = jax.random.randint(keys[1], (devices,), (3 * edges + 9) // 10, edges // 2 + 1)
    chosen = jax.random.randint(keys[2], (), 0, devices)
    live_count = jnp.where(jnp.arange(devices) == chosen, edges, 2 * halves)
    canon = jnp.arange(edges)[None, :]
    block_id = jnp.sum((canon[:, :, None] >= block_end[:, None, :]).astype(jnp.int32), axis=2)
    block_clip = jnp.minimum(block_id, list_count - 1)
    within = canon - jnp.take_along_axis(block_start, block_clip, axis=1)
    is_remote = canon < remote[:, None]
    is_live = canon < live_count[:, None]
    remote_value = edges + jnp.bitwise_xor(block_clip, 1) * CAP + within
    self_partner = remote[:, None] + jnp.bitwise_xor(canon - remote[:, None], 1)
    noise = jax.random.randint(keys[3], (devices, edges), 0, 2 ** 16) * edges + canon
    order_key = jnp.where(is_live, noise, 2 ** 16 * edges + canon)
    order = jnp.argsort(order_key, axis=1)
    new_place = jnp.argsort(order, axis=1).astype(jnp.int32)
    self_new = jnp.take_along_axis(new_place, jnp.clip(self_partner, 0, edges - 1), axis=1)
    rev_canon = jnp.where(is_remote, remote_value, jnp.where(is_live, self_new, -1))
    rev_new = jnp.zeros((devices, edges), jnp.int32)
    rev_new = jax.vmap(lambda target, placed, values: target.at[placed].set(values))(rev_new, new_place, rev_canon.astype(jnp.int32))
    pick_noise = jax.random.randint(keys[4], (devices, list_count, edges), 0, 2 ** 16) * edges + canon[:, None, :]
    in_block = (block_id[:, None, :] == jnp.arange(list_count)[None, :, None]) & is_remote[:, None, :]
    pick_key = jnp.where(in_block, within[:, None, :], jnp.where(is_live[:, None, :], edges + pick_noise, 2 ** 17 * edges + canon[:, None, :]))
    picked = jnp.argsort(pick_key, axis=2)[:, :, :CAP]
    send_lists = jax.vmap(lambda placed, chosen_rows: placed[chosen_rows])(new_place, picked)
    extra = jax.random.randint(keys[5], (devices, list_count), 1, CAP - pair_count + 1)
    counts = pair_count + extra
    full_device = jax.random.randint(keys[6], (), 0, devices)
    full_list = jax.random.randint(keys[7], (), 0, list_count)
    counts = jnp.where((jnp.arange(devices)[:, None] == full_device) & (jnp.arange(list_count)[None, :] == full_list), CAP, counts)
    arrive_count = jnp.stack([jnp.roll(counts[:, which], shifts[which], axis=0) for which in range(list_count)], axis=1)
    per_edge = jax.random.randint(keys[8], (devices, edges), K // 4, K + 1)
    lane = jax.random.randint(keys[9], (devices, edges, K), 0, 2 * list_count)
    local_pick = jax.random.randint(keys[10], (devices, edges, K), 0, live_count[:, None, None])
    block_pick = jnp.clip(lane - list_count, 0, list_count - 1)
    limit = jnp.take_along_axis(arrive_count, block_pick.reshape(devices, -1), axis=1).reshape(devices, edges, K)
    slot_pick = jax.random.randint(keys[11], (devices, edges, K), 0, limit)
    source = jnp.where(lane < list_count, local_pick, edges + block_pick * CAP + slot_pick)
    used = (jnp.arange(K)[None, None, :] < per_edge[:, :, None]) & (jnp.arange(edges)[None, :, None] < live_count[:, None, None])
    trips = jnp.where(used, source, -1)
    return (trips.reshape(devices * edges, K), send_lists.reshape(devices * list_count, CAP), counts.reshape(devices * list_count), rev_new.reshape(devices * edges), live_count)


def build_all(key):
    slab_keys = jax.random.split(jax.random.fold_in(key, 31), SLABS)
    return jax.vmap(build_slab)(slab_keys)


def draw_trip_src(key, part):
    return build_all(key)[0].astype(jnp.int32)


def draw_send_rows(key, part):
    return build_all(key)[1].astype(jnp.int32)


def draw_send_count(key, part):
    return build_all(key)[2].astype(jnp.int32)


def draw_rev_src(key, part):
    return build_all(key)[3].astype(jnp.int32)


def draw_edge_count(key, part):
    return build_all(key)[4].astype(jnp.int32)


def block_scale(rng, dims, shards, low, top_value):
    factor_of = 1.0
    for position, blocks in shards:
        steps = jax.random.uniform(jax.random.fold_in(jax.random.fold_in(rng, 6), position), (blocks,), jnp.float32, low / len(shards), top_value / len(shards))
        factor_of = factor_of * jnp.repeat(jnp.exp(steps), dims[position] // blocks).reshape((-1,) + (1,) * (len(dims) - 1 - position))
    return factor_of


def scatter_about(key, dims, deviation, reach, shards=(), kind=jnp.bfloat16):
    drawn = jax.random.normal(key, dims, jnp.float32) * deviation
    if len(shards) > 0:
        drawn = block_scale(key, dims, shards, -0.22, 0.18) * drawn
    return jnp.clip(drawn, min=-reach, max=reach).astype(kind)


def setup_inputs(seed: int = 0) -> dict:
    key_of = jax.random.split(jax.random.key(seed), 13)
    return {
        "messages": scatter_about(key_of[0], (SLABS, EDGES, D), 1.0, 6.0, ((0, 4), (1, 8))),
        "cotangent": scatter_about(key_of[1], (SLABS, EDGES, D), 1.0, 6.0, ((0, 4), (1, 8))),
        "triplet_basis": scatter_about(key_of[2], (SLABS, EDGES, K * NB), 1.0, 6.0, ((0, 4), (1, 8))),
        "w_edge": scatter_about(key_of[3], (D, D), D ** -0.5, 0.25),
        "w_down": scatter_about(key_of[4], (D, TW), D ** -0.5, 0.25),
        "w_bil": scatter_about(key_of[5], (NB, TW * TW), (NB * TW * K) ** -0.5, 0.01171875),
        "w_up": scatter_about(key_of[6], (2, TW, D), TW ** -0.5, 0.75),
        "trip_src": draw_trip_src(jax.random.fold_in(key_of[12], 71), 0),
        "send_rows": draw_send_rows(jax.random.fold_in(key_of[12], 71), 0),
        "send_count": draw_send_count(jax.random.fold_in(key_of[12], 71), 0),
        "rev_src": draw_rev_src(jax.random.fold_in(key_of[12], 71), 0),
        "edge_count": draw_edge_count(jax.random.fold_in(key_of[12], 71), 0),
    }


inv_root = 0.7071067811865476

def silu_slope(values):
    sigma = jax.nn.sigmoid(values)
    return sigma * (1.0 + values * (1.0 - sigma))

def offsets(count):
    return [(which // 2 + 1) * (1 - 2 * (which % 2)) for which in range(count)]

def contract(left, right):
    return lax.dot_general(left, right, (((0,), (0,)), ((), ())), preferred_element_type=jnp.float32)

def slab_terms(messages, cotangent, triplet_basis, w_edge, w_down, w_bil, w_up, trip_src, send_rows, send_count, rev_src, edge_count):
    list_count = 2 * REACH
    shifts = offsets(list_count)
    alive = jnp.arange(E_DEV)[None, :] < edge_count[:, None]
    pre_edge = jnp.dot(messages, w_edge, preferred_element_type=jnp.float32)
    hidden = jax.nn.silu(pre_edge).astype(jnp.bfloat16)
    pre_down = jnp.dot(hidden, w_down, preferred_element_type=jnp.float32)
    reduced = jax.nn.silu(pre_down).astype(jnp.bfloat16)
    list_rows = send_rows.reshape(N_GRAPH, list_count * CAP)
    filled = jnp.arange(CAP)[None, None, :] < send_count.reshape(N_GRAPH, list_count)[:, :, None]

    def pooled(values):
        columns = values.shape[-1]
        local = values.reshape(N_GRAPH, E_DEV, columns)
        sent = jax.vmap(lambda table, picks: table[picks])(local, list_rows)
        sent = sent.reshape(N_GRAPH, list_count, CAP, columns)
        sent = jnp.where(filled[:, :, :, None], sent, jnp.zeros((), values.dtype))
        blocks = [jnp.roll(sent[:, which], shifts[which], axis=0) for which in range(list_count)]
        return jnp.concatenate([local] + blocks, axis=1)
    pool_red = pooled(reduced)
    pool_cot = pooled(cotangent)
    trips = trip_src.reshape(N_GRAPH, E_DEV, K)
    revs = rev_src.reshape(N_GRAPH, E_DEV)
    bases = triplet_basis.reshape(N_GRAPH, E_DEV, K, NB)
    cots = cotangent.reshape(N_GRAPH, E_DEV, D)
    w_flat = w_bil.reshape(NB * TW, TW)

    def device_step(totals, item):
        pool_rows, pool_cots, basis, trip, reverse, own_cot, live_rows = item
        valid = trip >= 0
        gathered = jnp.where(valid[:, :, None], pool_rows[jnp.maximum(trip, 0)], jnp.zeros((), jnp.bfloat16))
        outer = jnp.einsum('ekb,ekc->ebc', basis.astype(jnp.float32), gathered.astype(jnp.float32))
        outer = outer.astype(jnp.bfloat16).reshape(E_DEV, NB * TW)
        state = jnp.dot(outer, w_flat, preferred_element_type=jnp.float32).astype(jnp.bfloat16)
        scaled = jnp.where(live_rows[:, None], own_cot.astype(jnp.float32) * inv_root, 0.0)
        pre_ca = jnp.dot(state, w_up[0], preferred_element_type=jnp.float32)
        grad_ca = (scaled * silu_slope(pre_ca)).astype(jnp.bfloat16)
        has_rev = reverse >= 0
        mirror = jnp.where(has_rev[:, None], pool_cots[jnp.maximum(reverse, 0)], jnp.zeros((), jnp.bfloat16))
        pre_ac = jnp.dot(state, w_up[1], preferred_element_type=jnp.float32)
        grad_ac = (mirror.astype(jnp.float32) * inv_root * silu_slope(pre_ac)).astype(jnp.bfloat16)
        up_ca = contract(state, grad_ca)
        up_ac = contract(state, grad_ac)
        back_rev = jnp.dot(grad_ac, w_up[1].T, preferred_element_type=jnp.float32).astype(jnp.bfloat16)
        back_rev = lax.optimization_barrier(back_rev).astype(jnp.float32)
        grad_state = (jnp.dot(grad_ca, w_up[0].T, preferred_element_type=jnp.float32) + back_rev).astype(jnp.bfloat16)
        grad_outer = jnp.dot(grad_state, w_flat.T, preferred_element_type=jnp.float32).astype(jnp.bfloat16)
        bil = contract(outer, grad_state)
        grad_trip = jnp.einsum('ebc,ekb->ekc', grad_outer.reshape(E_DEV, NB, TW).astype(jnp.float32), basis.astype(jnp.float32))
        grad_trip = jnp.where(valid[:, :, None], grad_trip, 0.0)
        grad_pool = jnp.zeros((POOL, TW), jnp.float32).at[jnp.maximum(trip, 0).reshape(-1)].add(grad_trip.reshape(-1, TW))
        return ((totals[0] + up_ca, totals[1] + up_ac, totals[2] + bil), grad_pool)
    start = (jnp.zeros((TW, D), jnp.float32), jnp.zeros((TW, D), jnp.float32), jnp.zeros((NB * TW, TW), jnp.float32))
    totals, grad_pool = lax.scan(device_step, start, (pool_red, pool_cot, bases, trips, revs, cots, alive))
    returned = grad_pool[:, E_DEV:].reshape(N_GRAPH, list_count, CAP, TW).astype(jnp.bfloat16)
    returned = lax.optimization_barrier(returned)
    grad_red = grad_pool[:, :E_DEV]
    rows_split = list_rows.reshape(N_GRAPH, list_count, CAP)
    for which in range(list_count):
        back = jnp.roll(returned[:, which], -shifts[which], axis=0).astype(jnp.float32)
        back = jnp.where(filled[:, which, :, None], back, 0.0)
        grad_red = jax.vmap(lambda target, picks, addend: target.at[picks].add(addend))(grad_red, rows_split[:, which], back)
    grad_red = grad_red.reshape(EDGES, TW)
    grad_down = (grad_red * silu_slope(pre_down)).astype(jnp.bfloat16)
    down_sum = contract(hidden, grad_down)
    grad_hidden = jnp.dot(grad_down, w_down.T, preferred_element_type=jnp.float32)
    grad_edge = (grad_hidden * silu_slope(pre_edge)).astype(jnp.bfloat16)
    edge_sum = contract(messages, grad_edge)
    grad_messages = jnp.dot(grad_edge, w_edge.T, preferred_element_type=jnp.float32).astype(jnp.bfloat16)
    return (grad_messages, edge_sum, down_sum, totals[2], jnp.stack([totals[0], totals[1]]))

def reference(messages, cotangent, triplet_basis, w_edge, w_down, w_bil, w_up, trip_src, send_rows, send_count, rev_src, edge_count):
    outputs = []
    edge_total = jnp.zeros((D, D), jnp.float32)
    down_total = jnp.zeros((D, TW), jnp.float32)
    bil_total = jnp.zeros((NB * TW, TW), jnp.float32)
    up_total = jnp.zeros((2, TW, D), jnp.float32)
    for slab in range(SLABS):
        grad_messages, edge_sum, down_sum, bil, up_sum = slab_terms(messages[slab], cotangent[slab], triplet_basis[slab], w_edge, w_down, w_bil, w_up, trip_src[slab], send_rows[slab], send_count[slab], rev_src[slab], edge_count[slab])
        outputs.append(grad_messages)
        edge_total = edge_total + edge_sum
        down_total = down_total + down_sum
        bil_total = bil_total + bil
        up_total = up_total + up_sum
    factor = 1.0 / jnp.sqrt(jnp.float32(SLABS * EDGES))
    return (jnp.stack(outputs), edge_total * factor, down_total * factor, bil_total.reshape(NB, TW * TW) * factor, up_total * factor)
```

```python
import functools
import math

import jax
import jax.numpy as jnp
from jax import lax
from jax.experimental import pallas as pl
from jax.experimental.pallas import tpu as pltpu
from jax.sharding import PartitionSpec as P

inv_root = 0.7071067811865476
bf16 = jnp.bfloat16
f32 = jnp.float32
GROUP = 8
NN = (((1,), (0,)), ((), ()))
NT = (((1,), (1,)), ((), ()))
TN = (((0,), (0,)), ((), ()))


def mm(left, right, dims=NN):
    return lax.dot_general(left, right, dims, preferred_element_type=f32)


def silu_slope(values):
    sigma = jax.nn.sigmoid(values)
    return sigma * (1.0 + values * (1.0 - sigma))


def offsets(count):
    return [(which // 2 + 1) * (1 - 2 * (which % 2)) for which in range(count)]


def shifted(block, axis, distance):
    devices = range(lax.axis_size(axis))
    route = [((i - distance) % len(devices), i) for i in devices]
    return lax.ppermute(block, axis, route)


def iota(shape, dim):
    return lax.broadcasted_iota(jnp.int32, shape, dim)


def one_hot(index, shape, dim):
    return jnp.where(index == iota(shape, dim), 1.0, 0.0).astype(bf16)


def vmem():
    return pl.BlockSpec(memory_space=pltpu.VMEM)


def params(**extra):
    return pltpu.CompilerParams(vmem_limit_bytes=60 * 1024 * 1024, **extra)


def send_hot(rows_ref, count_ref, which, edges):
    capacity = rows_ref.shape[2]
    rows = rows_ref[0, which : which + 1, :]
    used = iota((1, capacity), 1) < count_ref[0, which]
    return one_hot(jnp.where(used, rows, -1), (edges, capacity), 0)


def front_kernel(
    count_ref, x_ref, we_ref, wd_ref, rows_ref, pre_ref, hid_ref, pdt_ref, red_ref, *send_refs
):
    edges = x_ref.shape[1]
    step = 256
    for start in range(0, edges, step):
        pre = mm(x_ref[0, start : start + step, :], we_ref[...])
        pre_ref[start : start + step, :] = pre
        hidden = (pre * jax.nn.sigmoid(pre)).astype(bf16)
        hid_ref[start : start + step, :] = hidden
        down = lax.dot_general(
            wd_ref[...], hidden, (((0,), (1,)), ((), ())), preferred_element_type=f32
        )
        pdt_ref[:, start : start + step] = down
        red_ref[:, start : start + step] = (down * jax.nn.sigmoid(down)).astype(bf16)
    for which, send_ref in enumerate(send_refs):
        hot = send_hot(rows_ref, count_ref, which, edges)
        send_ref[...] = mm(red_ref[...], hot).astype(bf16)


def smem():
    return pl.BlockSpec(memory_space=pltpu.SMEM)


def front(messages, w_edge, w_down, rows, counts):
    _, edges, model = messages.shape
    narrow = w_down.shape[1]
    _, lists, capacity = rows.shape
    return pl.pallas_call(
        front_kernel,
        out_shape=(
            jax.ShapeDtypeStruct((edges, model), f32),
            jax.ShapeDtypeStruct((edges, model), bf16),
            jax.ShapeDtypeStruct((narrow, edges), f32),
            jax.ShapeDtypeStruct((narrow, edges), bf16),
        )
        + (jax.ShapeDtypeStruct((narrow, capacity), bf16),) * lists,
        in_specs=[smem()] + [vmem()] * 4,
        out_specs=(vmem(),) * (4 + lists),
        compiler_params=params(),
        name="front",
    )(counts, messages, w_edge, w_down, rows)


def pick_kernel(count_ref, cot_ref, rows_ref, after_ref, *send_refs):
    edges = cot_ref.shape[1]
    for which, send_ref in enumerate(send_refs):
        hot = send_hot(rows_ref, count_ref, which, edges)
        send_ref[...] = mm(hot, cot_ref[0], TN).astype(bf16)


def pick(cotangent, rows, counts, after):
    _, edges, model = cotangent.shape
    _, lists, capacity = rows.shape
    return pl.pallas_call(
        pick_kernel,
        out_shape=(jax.ShapeDtypeStruct((capacity, model), bf16),) * lists,
        in_specs=[smem(), vmem(), vmem(), pl.BlockSpec(memory_space=pl.ANY)],
        out_specs=(vmem(),) * lists,
        compiler_params=params(),
        name="pick",
    )(counts, cotangent, rows, after)


def widen_weights(wb_ref, wide):
    basis, _ = wb_ref.shape
    narrow = wide.shape[1]
    padded = wide.shape[0] // narrow
    zeros = jnp.zeros((padded - basis, narrow), bf16)
    for c in range(0, narrow, 2):
        pair = wb_ref[:, c * narrow : (c + 2) * narrow]
        wide[c * padded : (c + 1) * padded, :] = jnp.concatenate(
            [pair[:, :narrow], zeros], axis=0
        )
        wide[(c + 1) * padded : (c + 2) * padded, :] = jnp.concatenate(
            [pair[:, narrow:], zeros], axis=0
        )


def split_index(trip, capacity):
    return jnp.bitwise_and(trip, capacity - 1), jnp.right_shift(
        trip, capacity.bit_length() - 1
    )


def forward_kernel(
    basis_count, sub, lists, basis_ref, trip_ref, red_ref, wb_ref, *rest
):
    recv_refs = rest[:lists]
    outer_ref, bas_ref, state_ref, pool, wide, slot_s, turn_s = rest[lists:]
    narrow, edges = red_ref.shape
    capacity = recv_refs[0].shape[1]
    rho = trip_ref.shape[1]
    slots = rho // GROUP
    padded = bas_ref.shape[1]
    locals_ = edges // capacity
    half = GROUP // 2

    @pl.when(pl.program_id(0) == 0)
    def _():
        for h in range(locals_):
            pool[h * narrow : (h + 1) * narrow, :] = red_ref[:, h * capacity : (h + 1) * capacity]
        for h in range(lists):
            pool[(locals_ + h) * narrow : (locals_ + h + 1) * narrow, :] = recv_refs[h][...]
        widen_weights(wb_ref, wide)

    groups = sub // GROUP
    lane = iota((1, rho), 1) % half
    row_half = iota((rho, padded), 0) % GROUP < half

    def body(index, carry):
        first = pl.multiple_of(index * sub, sub)
        first_group = pl.multiple_of(index * groups, groups)
        x = basis_ref[0, pl.ds(first, sub), :].astype(f32)
        for k in range(slots):
            tile, off = divmod(k * basis_count, 128)
            if off + basis_count <= 128:
                part = x[:, tile * 128 : tile * 128 + 128]
                if off:
                    part = pltpu.roll(part, 128 - off, 1)
            else:
                part = pltpu.roll(x[:, tile * 128 : tile * 128 + 256], 256 - off, 1)[:, :128]
            for g in range(groups):
                slot_s[g, k * GROUP : (k + 1) * GROUP, :] = part[g * GROUP : (g + 1) * GROUP, :]
        for g in range(groups):
            bas = slot_s[g].astype(bf16)
            bas_ref[pl.ds((first_group + g) * rho, rho), :] = bas
            lo, hi = split_index(trip_ref[pl.ds(first_group + g, 1), :], capacity)
            hot = one_hot(lo, (capacity, rho), 0)
            found = mm(pool[...], hot)
            gathered = jnp.zeros((narrow, rho), f32)
            for h in range(locals_ + lists):
                gathered = gathered + jnp.where(
                    hi == h, found[h * narrow : (h + 1) * narrow, :], 0.0
                )
            spread = jnp.concatenate(
                [jnp.where(lane == e, gathered, 0.0).astype(bf16) for e in range(half)], axis=0
            )
            zero = jnp.zeros_like(bas)
            pairs = jnp.concatenate(
                [jnp.where(row_half, bas, zero), jnp.where(row_half, zero, bas)], axis=1
            )
            outer = mm(spread, pairs)
            turn_s[g, : half * narrow, :] = outer[:, :padded]
            turn_s[g, half * narrow :, :] = outer[:, padded:]
        for g in range(0, groups, 2):
            for c in range(narrow):
                block = jnp.concatenate(
                    [
                        turn_s[g, pl.ds(c, GROUP, stride=narrow), :],
                        turn_s[g + 1, pl.ds(c, GROUP, stride=narrow), :],
                    ],
                    axis=0,
                )
                outer_ref[
                    pl.ds(pl.multiple_of(first + g * GROUP, 2 * GROUP), 2 * GROUP),
                    c * padded : (c + 1) * padded,
                ] = block.astype(bf16)
        return carry

    lax.fori_loop(0, outer_ref.shape[0] // sub, body, 0)
    state_ref[...] = mm(outer_ref[...], wide[...]).astype(bf16)


def forward(triplet_basis, trips, red, recv, w_bil):
    narrow, edges = red.shape
    lists = len(recv)
    capacity = recv[0].shape[1]
    basis_count = w_bil.shape[0]
    rho = trips.shape[1]
    padded = 128
    block = 256
    sub = 64
    steps = edges // block
    resident = lambda *shape: pl.BlockSpec(shape, lambda i: (0,) * len(shape))
    return pl.pallas_call(
        functools.partial(forward_kernel, basis_count, sub, lists),
        grid=(steps,),
        out_shape=(
            jax.ShapeDtypeStruct((edges, narrow * padded), bf16),
            jax.ShapeDtypeStruct((edges * rho // GROUP, padded), bf16),
            jax.ShapeDtypeStruct((edges, narrow), bf16),
        ),
        in_specs=[
            pl.BlockSpec((1, block, triplet_basis.shape[2]), lambda i: (0, i, 0)),
            pl.BlockSpec((block // GROUP, rho), lambda i: (i, 0)),
            resident(narrow, edges),
            resident(*w_bil.shape),
        ]
        + [resident(narrow, capacity)] * lists,
        out_specs=(
            pl.BlockSpec((block, narrow * padded), lambda i: (i, 0)),
            pl.BlockSpec((block * rho // GROUP, padded), lambda i: (i, 0)),
            pl.BlockSpec((block, narrow), lambda i: (i, 0)),
        ),
        scratch_shapes=[
            pltpu.VMEM((edges // capacity * narrow + lists * narrow, capacity), bf16),
            pltpu.VMEM((narrow * padded, narrow), bf16),
            pltpu.VMEM((sub // GROUP, rho, padded), f32),
            pltpu.VMEM((sub // GROUP, GROUP * narrow, padded), f32),
        ],
        compiler_params=params(),
        name="forward",
    )(triplet_basis, trips, red, w_bil, *recv)


def state_kernel(
    scale, parts, lists,
    count_ref, outer_ref, state_ref, cot_ref, rev_ref, own_ref, wu_ref, *rest
):
    recv_refs = rest[:lists]
    grad_ref, share_ref, ca_s, ac_s, bil_s = rest[lists:]
    block, narrow = state_ref.shape
    edges = own_ref.shape[1]
    capacity, model = recv_refs[0].shape
    columns = outer_ref.shape[1]
    pid = pl.program_id(0)

    @pl.when(pid == 0)
    def _():
        ca_s[...] = jnp.zeros_like(ca_s)
        ac_s[...] = jnp.zeros_like(ac_s)
        bil_s[...] = jnp.zeros_like(bil_s)

    state = state_ref[...]
    alive = pid * block + iota((block, 1), 0) < count_ref[0, 0]
    scaled = jnp.where(alive, cot_ref[0].astype(f32) * inv_root, 0.0)
    pre_ca = mm(state, wu_ref[0])
    grad_ca = (scaled * silu_slope(pre_ca)).astype(bf16)
    reverse = rev_ref[...]
    mirror = mm(one_hot(reverse, (edges, block), 0), own_ref[0], TN)
    for which, recv_ref in enumerate(recv_refs):
        base = edges + which * capacity
        mirror = mirror + mm(one_hot(reverse - base, (capacity, block), 0), recv_ref[...], TN)
    pre_ac = mm(state, wu_ref[1])
    grad_ac = (mirror * inv_root * silu_slope(pre_ac)).astype(bf16)
    ca_s[...] += mm(grad_ca, state, TN)
    ac_s[...] += mm(grad_ac, state, TN)
    back_rev = mm(grad_ac, wu_ref[1], NT).astype(bf16).astype(f32)
    grad_state = (mm(grad_ca, wu_ref[0], NT) + back_rev).astype(bf16)
    grad_ref[...] = grad_state
    wide_step = 1024
    for start in range(0, columns, wide_step):
        bil_s[:, start : start + wide_step] += mm(
            grad_state, outer_ref[:, start : start + wide_step], TN
        )

    @pl.when(pid == pl.num_programs(0) - 1)
    def _():
        dests, height, _ = share_ref.shape
        slabs = dests // parts
        span = columns // parts
        thin = model // dests
        both = jnp.concatenate([ca_s[...], ac_s[...]], axis=1) * scale
        for slab in range(slabs):
            for part in range(parts):
                dest = slab * parts + part
                share_ref[dest, :, :span] = (
                    bil_s[slab * height : (slab + 1) * height, part * span : (part + 1) * span]
                    * scale
                ).astype(bf16)
                first = (part * slabs + slab) * thin
                piece = both[first : first + thin, :]
                if thin < height:
                    piece = jnp.concatenate(
                        [piece, jnp.zeros((height - thin, 2 * narrow), f32)], axis=0
                    )
                share_ref[dest, :, span:] = piece.astype(bf16)


def state_grads(count, outer, state, cotangent, rev, recv_cot, w_up, scale, parts, slabs):
    edges, narrow = state.shape
    model = cotangent.shape[2]
    columns = outer.shape[1]
    block = 256
    lists = len(recv_cot)
    height = narrow // slabs
    share = (parts * slabs, height, columns // parts + 2 * narrow)
    resident = lambda *shape: pl.BlockSpec(shape, lambda i: (0,) * len(shape))
    return pl.pallas_call(
        functools.partial(state_kernel, scale, parts, lists),
        grid=(edges // block,),
        out_shape=(
            jax.ShapeDtypeStruct((edges, narrow), bf16),
            jax.ShapeDtypeStruct(share, bf16),
        ),
        in_specs=[
            smem(),
            pl.BlockSpec((block, columns), lambda i: (i, 0)),
            pl.BlockSpec((block, narrow), lambda i: (i, 0)),
            pl.BlockSpec((1, block, model), lambda i: (0, i, 0)),
            pl.BlockSpec((1, block), lambda i: (0, i)),
            resident(1, edges, model),
            resident(*w_up.shape),
        ]
        + [resident(*recv_cot[0].shape)] * lists,
        out_specs=(
            pl.BlockSpec((block, narrow), lambda i: (i, 0)),
            resident(*share),
        ),
        scratch_shapes=[
            pltpu.VMEM((model, narrow), f32),
            pltpu.VMEM((model, narrow), f32),
            pltpu.VMEM((narrow, columns), f32),
        ],
        compiler_params=params(),
        name="state_grads",
    )(count, outer, state, cotangent, rev, cotangent, w_up, *recv_cot)


def backward_kernel(
    sub, lists, bas_ref, grad_ref, trip_ref, wb_ref, home_ref, *rest
):
    back_refs = rest[:lists]
    pool_s, wide, turn_s, cast_s, hot_s = rest[lists:]
    block, narrow = grad_ref.shape
    padded = bas_ref.shape[1]
    rho = trip_ref.shape[1]
    rows, capacity = pool_s.shape
    half = GROUP // 2
    pid = pl.program_id(0)

    @pl.when(pid == 0)
    def _():
        widen_weights(wb_ref, wide)
        pool_s[...] = jnp.zeros_like(pool_s)

    grad_state = grad_ref[...]

    def spread(pair, carry):
        start = pl.multiple_of(pair * 2 * padded, 2 * padded)
        grad = mm(grad_state, wide[pl.ds(start, 2 * padded), :], NT)
        for g in range(block // GROUP):
            for side in range(2):
                turn_s[pl.ds(g * GROUP * narrow + 2 * pair + side, GROUP, stride=narrow), :] = grad[
                    g * GROUP : (g + 1) * GROUP, side * padded : (side + 1) * padded
                ]
        return carry

    lax.fori_loop(0, narrow // 2, spread, 0)
    groups = sub // GROUP
    lane = iota((1, rho), 1) % half
    row_half = iota((rho, padded), 0) % GROUP < half

    def body(index, carry):
        first_group = pl.multiple_of(index * groups, groups)
        for g in range(groups):
            here = first_group + g
            base = pl.multiple_of(here * GROUP * narrow, GROUP * narrow)
            bas = bas_ref[pl.ds(pl.multiple_of(here * rho, rho), rho), :]
            zero = jnp.zeros_like(bas)
            pairs = jnp.concatenate(
                [jnp.where(row_half, bas, zero), jnp.where(row_half, zero, bas)], axis=1
            )
            grads = jnp.concatenate(
                [
                    turn_s[pl.ds(base, half * narrow), :],
                    turn_s[pl.ds(base + half * narrow, half * narrow), :],
                ],
                axis=1,
            ).astype(bf16)
            mixed = mm(grads, pairs, NT)
            trip_grad = jnp.zeros((narrow, rho), f32)
            for e in range(half):
                trip_grad = trip_grad + jnp.where(
                    lane == e, mixed[e * narrow : (e + 1) * narrow, :], 0.0
                )
            lo, hi = split_index(trip_ref[pl.ds(here, 1), :], capacity)
            hot_s[:, g * rho : (g + 1) * rho] = one_hot(lo, (capacity, rho), 0)
            for h in range(rows // narrow):
                cast_s[h * narrow : (h + 1) * narrow, g * rho : (g + 1) * rho] = jnp.where(
                    hi == h, trip_grad, 0.0
                ).astype(bf16)
        pool_s[...] += mm(cast_s[...], hot_s[...], NT)
        return carry

    lax.fori_loop(0, block // sub, body, 0)

    @pl.when(pid == pl.num_programs(0) - 1)
    def _():
        home = home_ref.shape[0]
        home_ref[...] = pool_s[:home, :]
        for which, back_ref in enumerate(back_refs):
            first = home + which * narrow
            back_ref[...] = pool_s[first : first + narrow, :].astype(bf16)


def backward(bas, grad_state, trips, w_bil, capacity, lists):
    edges, narrow = grad_state.shape
    rho = trips.shape[1]
    padded = bas.shape[1]
    block = 256
    sub = 64
    home = edges // capacity * narrow
    rows = home + lists * narrow
    resident = lambda *shape: pl.BlockSpec(shape, lambda i: (0,) * len(shape))
    return pl.pallas_call(
        functools.partial(backward_kernel, sub, lists),
        grid=(edges // block,),
        out_shape=(jax.ShapeDtypeStruct((home, capacity), f32),)
        + (jax.ShapeDtypeStruct((narrow, capacity), bf16),) * lists,
        in_specs=[
            pl.BlockSpec((block * rho // GROUP, padded), lambda i: (i, 0)),
            pl.BlockSpec((block, narrow), lambda i: (i, 0)),
            pl.BlockSpec((block // GROUP, rho), lambda i: (i, 0)),
            resident(*w_bil.shape),
        ],
        out_specs=(resident(home, capacity),) + (resident(narrow, capacity),) * lists,
        scratch_shapes=[
            pltpu.VMEM((rows, capacity), f32),
            pltpu.VMEM((narrow * padded, narrow), bf16),
            pltpu.VMEM((block * narrow, padded), f32),
            pltpu.VMEM((rows, sub // GROUP * rho), bf16),
            pltpu.VMEM((capacity, sub // GROUP * rho), bf16),
        ],
        compiler_params=params(),
        name="backward",
    )(bas, grad_state, trips, w_bil)


def tail_kernel(
    scale, parts, lists,
    count_ref, pool_ref, rows_ref, pdt_ref, pre_ref, hid_ref, x_ref, we_ref, wd_ref, *rest
):
    back_refs = rest[:lists]
    out_ref, share_ref, grad_s = rest[lists:]
    narrow, edges = pdt_ref.shape
    capacity = back_refs[0].shape[1]
    model = pre_ref.shape[1]
    grad = jnp.concatenate(
        [pool_ref[h * narrow : (h + 1) * narrow, :] for h in range(edges // capacity)], axis=1
    )
    for which, back_ref in enumerate(back_refs):
        grad = grad + mm(back_ref[...], send_hot(rows_ref, count_ref, which, edges), NT)
    grad_down = (grad * silu_slope(pdt_ref[...])).astype(bf16)
    step = 256
    for start in range(0, edges, step):
        part = slice(start, start + step)
        grad_hidden = lax.dot_general(
            grad_down[:, part], wd_ref[...], (((0,), (1,)), ((), ())), preferred_element_type=f32
        )
        grad_edge = (grad_hidden * silu_slope(pre_ref[part, :])).astype(bf16)
        grad_s[part, :] = grad_edge
        out_ref[0, part, :] = mm(grad_edge, we_ref[...], NT).astype(bf16)
    dests, height, _ = share_ref.shape
    slabs = dests // parts
    down = lax.dot_general(
        hid_ref[...], grad_down, (((0,), (1,)), ((), ())), preferred_element_type=f32
    )
    down = jnp.concatenate([down, jnp.zeros_like(down)], axis=1)
    span = model // parts
    for start in range(0, model, step):
        both = (
            jnp.concatenate(
                [
                    mm(x_ref[0, :, start : start + step], grad_s[...], TN),
                    down[start : start + step, :],
                ],
                axis=1,
            )
            * scale
        ).astype(bf16)
        for first in range(start, start + step, height):
            part, slab = first // span, first % span // height
            share_ref[slab * parts + part] = both[first - start : first - start + height, :]


def tail(pool, back, rows, counts, pdt, pre, hidden, messages, w_edge, w_down, scale, parts, slabs):
    _, edges, model = messages.shape
    narrow = w_down.shape[1]
    dests = parts * slabs
    return pl.pallas_call(
        functools.partial(tail_kernel, scale, parts, len(back)),
        out_shape=(
            jax.ShapeDtypeStruct((1, edges, model), bf16),
            jax.ShapeDtypeStruct((dests, model // dests, model + 2 * narrow), bf16),
        ),
        in_specs=[smem()] + [vmem()] * (8 + len(back)),
        out_specs=(vmem(),) * 2,
        scratch_shapes=[pltpu.VMEM((edges, model), bf16)],
        compiler_params=params(),
        name="tail",
    )(counts, pool, rows, pdt, pre, hidden, messages, w_edge, w_down, *back)


def add_kernel(thin, *refs):
    *in_refs, out_ref = refs
    copies = out_ref.shape[0]
    at = 0
    for in_ref in in_refs:
        dests, height, wide = in_ref.shape
        total = in_ref[0].astype(f32)
        for dest in range(1, dests):
            total = total + in_ref[dest].astype(f32)
        total = total.astype(bf16)
        for copy in range(copies):
            out_ref[copy, :height, at : at + wide] = total
            if height < out_ref.shape[1]:
                out_ref[copy, height:, at : at + wide] = jnp.zeros(
                    (out_ref.shape[1] - height, wide), bf16
                )
        at += wide


def add_shares(early, late, copies):
    height = max(early.shape[1], late.shape[1])
    return pl.pallas_call(
        functools.partial(add_kernel, 0),
        out_shape=jax.ShapeDtypeStruct((copies, height, early.shape[2] + late.shape[2]), bf16),
        in_specs=[vmem()] * 2,
        out_specs=vmem(),
        compiler_params=params(),
        name="add_shares",
    )(early, late)


def finish_kernel(thin, in_ref, edge_ref, down_ref, bil_ref, up_ref):
    slabs, height, _ = in_ref.shape
    basis = bil_ref.shape[0]
    _, narrow, _ = up_ref.shape
    padded = 128
    span = bil_ref.shape[1] // narrow * padded
    model = edge_ref.shape[1]
    taken = narrow // slabs
    for c in range(bil_ref.shape[1] // narrow):
        block = jnp.concatenate(
            [in_ref[s, :taken, c * padded : (c + 1) * padded] for s in range(slabs)], axis=0
        ).astype(f32)
        bil_ref[:, c * narrow : (c + 1) * narrow] = block.T[:basis, :]
    both = jnp.concatenate([in_ref[s, :thin, span : span + 2 * narrow] for s in range(slabs)], axis=0)
    both = both.astype(f32).T
    up_ref[0] = both[:narrow, :]
    up_ref[1] = both[narrow:, :]
    at = span + 2 * narrow
    for s in range(slabs):
        part = slice(s * thin, (s + 1) * thin)
        edge_ref[part, :] = in_ref[s, :thin, at : at + model].astype(f32)
        down_ref[part, :] = in_ref[s, :thin, at + model : at + model + narrow].astype(f32)


def finish(shares, basis, narrow, model, parts):
    slabs = shares.shape[0]
    rows = model // parts
    return pl.pallas_call(
        functools.partial(finish_kernel, rows // slabs),
        out_shape=(
            jax.ShapeDtypeStruct((rows, model), f32),
            jax.ShapeDtypeStruct((rows, narrow), f32),
            jax.ShapeDtypeStruct((basis, narrow * narrow // parts), f32),
            jax.ShapeDtypeStruct((2, narrow, rows), f32),
        ),
        in_specs=[vmem()],
        out_specs=(vmem(),) * 4,
        compiler_params=params(),
        name="finish",
    )(shares)


def body(
    messages,
    cotangent,
    triplet_basis,
    w_edge,
    w_down,
    w_bil,
    w_up,
    trip_src,
    send_rows,
    send_count,
    rev_src,
    edge_count,
):
    _, edges, model = messages.shape
    narrow = w_down.shape[1]
    slots = trip_src.shape[2]
    _, lists, capacity = send_rows.shape
    basis_count = w_bil.shape[0]
    parts = lax.axis_size("graph")
    slabs = lax.axis_size("dp")
    scale = 1.0 / math.sqrt(slabs * parts * edges)
    shifts = offsets(lists)
    trips = (
        trip_src[0]
        .reshape(edges // GROUP, GROUP, slots)
        .transpose(0, 2, 1)
        .reshape(edges // GROUP, GROUP * slots)
    )
    pre, hidden, pdt, red, *send_red = front(messages, w_edge, w_down, send_rows, send_count)
    recv_red = [shifted(send_red[w], "graph", shifts[w]) for w in range(lists)]
    send_cot = pick(cotangent, send_rows, send_count, red)
    recv_cot = [shifted(send_cot[w], "graph", shifts[w]) for w in range(lists)]
    outer, bas, state = forward(triplet_basis, trips, red, recv_red, w_bil)
    grad_state, early = state_grads(
        edge_count, outer, state, cotangent, rev_src, recv_cot, w_up, scale, parts, slabs
    )
    early = lax.all_to_all(early, ("dp", "graph"), 0, 0)
    home, *returned = backward(bas, grad_state, trips, w_bil, capacity, lists)
    back = [shifted(returned[w], "graph", -shifts[w]) for w in range(lists)]
    grad_messages, late = tail(
        home, back, send_rows, send_count, pdt, pre, hidden, messages, w_edge, w_down,
        scale, parts, slabs,
    )
    late = lax.all_to_all(late, ("dp", "graph"), 0, 0)
    shares = lax.all_to_all(add_shares(early, late, slabs), "dp", 0, 0)
    edge_out, down_out, bil_out, up_out = finish(shares, basis_count, narrow, model, parts)
    return (grad_messages, edge_out, down_out, bil_out, up_out)


def solution(mesh):
    return jax.shard_map(
        body,
        mesh=mesh,
        in_specs=(
            P("dp", "graph", None),
            P("dp", "graph", None),
            P("dp", "graph", None),
            P(),
            P(),
            P(),
            P(),
            P("dp", "graph", None),
            P("dp", "graph", None),
            P("dp", "graph"),
            P("dp", "graph"),
            P("dp", "graph"),
        ),
        out_specs=(
            P("dp", "graph", None),
            P("graph", None),
            P("graph", None),
            P(None, "graph"),
            P(None, None, "graph"),
        ),
        check_vma=False,
    )
```

```python
import functools
import math

import jax
import jax.numpy as jnp
from jax import lax
from jax.experimental import pallas as pl
from jax.experimental.pallas import tpu as pltpu
from jax.sharding import PartitionSpec as P


inv_root = 0.7071067811865476
bf16 = jnp.bfloat16
f32 = jnp.float32
GROUP = 8
NN = (((1,), (0,)), ((), ()))
NT = (((1,), (1,)), ((), ()))
TN = (((0,), (0,)), ((), ()))


def mm(left, right, dims=NN):
    return lax.dot_general(left, right, dims, preferred_element_type=f32)


def silu_slope(values):
    sigma = jax.nn.sigmoid(values)
    return sigma * (1.0 + values * (1.0 - sigma))


def offsets(count):
    return [(which // 2 + 1) * (1 - 2 * (which % 2)) for which in range(count)]


def shifted(block, axis, distance):
    devices = range(lax.axis_size(axis))
    route = [((i - distance) % len(devices), i) for i in devices]
    return lax.ppermute(block, axis, route)


def iota(shape, dim):
    return lax.broadcasted_iota(jnp.int32, shape, dim)


def one_hot(index, shape, dim):
    return jnp.where(index == iota(shape, dim), 1.0, 0.0).astype(bf16)


def vmem():
    return pl.BlockSpec(memory_space=pltpu.VMEM)


def params(**extra):
    return pltpu.CompilerParams(vmem_limit_bytes=60 * 1024 * 1024, **extra)


def send_hot(rows_ref, count_ref, which, edges):
    capacity = rows_ref.shape[2]
    rows = rows_ref[0, which : which + 1, :]
    used = iota((1, capacity), 1) < count_ref[0, which]
    return one_hot(jnp.where(used, rows, -1), (edges, capacity), 0)


def front_kernel(
    count_ref, x_ref, we_ref, wd_ref, rows_ref, pre_ref, hid_ref, pdt_ref, red_ref, *send_refs
):
    edges = x_ref.shape[1]
    step = 256
    for start in range(0, edges, step):
        pre = mm(x_ref[0, start : start + step, :], we_ref[...])
        pre_ref[start : start + step, :] = pre
        hidden = (pre * jax.nn.sigmoid(pre)).astype(bf16)
        hid_ref[start : start + step, :] = hidden
        down = lax.dot_general(
            wd_ref[...], hidden, (((0,), (1,)), ((), ())), preferred_element_type=f32
        )
        pdt_ref[:, start : start + step] = down
        red_ref[:, start : start + step] = (down * jax.nn.sigmoid(down)).astype(bf16)
    for which, send_ref in enumerate(send_refs):
        hot = send_hot(rows_ref, count_ref, which, edges)
        send_ref[...] = mm(red_ref[...], hot).astype(bf16)


def smem():
    return pl.BlockSpec(memory_space=pltpu.SMEM)


def front(messages, w_edge, w_down, rows, counts):
    _, edges, model = messages.shape
    narrow = w_down.shape[1]
    _, lists, capacity = rows.shape
    return pl.pallas_call(
        front_kernel,
        out_shape=(
            jax.ShapeDtypeStruct((edges, model), f32),
            jax.ShapeDtypeStruct((edges, model), bf16),
            jax.ShapeDtypeStruct((narrow, edges), f32),
            jax.ShapeDtypeStruct((narrow, edges), bf16),
        )
        + (jax.ShapeDtypeStruct((narrow, capacity), bf16),) * lists,
        in_specs=[smem()] + [vmem()] * 4,
        out_specs=(vmem(),) * (4 + lists),
        compiler_params=params(),
        name="front",
    )(counts, messages, w_edge, w_down, rows)


def pick_kernel(count_ref, cot_ref, rows_ref, after_ref, *send_refs):
    edges = cot_ref.shape[1]
    for which, send_ref in enumerate(send_refs):
        hot = send_hot(rows_ref, count_ref, which, edges)
        send_ref[...] = mm(hot, cot_ref[0], TN).astype(bf16)


def pick(cotangent, rows, counts, after):
    _, _, model = cotangent.shape
    _, lists, capacity = rows.shape
    return pl.pallas_call(
        pick_kernel,
        out_shape=(jax.ShapeDtypeStruct((capacity, model), bf16),) * lists,
        in_specs=[smem(), vmem(), vmem(), pl.BlockSpec(memory_space=pl.ANY)],
        out_specs=(vmem(),) * lists,
        compiler_params=params(),
        name="pick",
    )(counts, cotangent, rows, after)


def widen_weights(wb_ref, wide):
    basis, _ = wb_ref.shape
    narrow = wide.shape[1]
    padded = wide.shape[0] // narrow
    zeros = jnp.zeros((padded - basis, narrow), bf16)
    for c in range(0, narrow, 2):
        pair = wb_ref[:, c * narrow : (c + 2) * narrow]
        wide[c * padded : (c + 1) * padded, :] = jnp.concatenate(
            [pair[:, :narrow], zeros], axis=0
        )
        wide[(c + 1) * padded : (c + 2) * padded, :] = jnp.concatenate(
            [pair[:, narrow:], zeros], axis=0
        )


def split_index(trip, capacity):
    low = jnp.bitwise_and(trip, capacity - 1).astype(f32).astype(bf16)
    return low, jnp.right_shift(trip, capacity.bit_length() - 1)


def low_iota(capacity, rho):
    return iota((capacity, rho), 0).astype(f32).astype(bf16)


def low_hot(low, numbers):
    one, zero = jnp.ones((), bf16), jnp.zeros((), bf16)
    return jnp.where(low == numbers, one, zero)


def align_kernel(basis_count, sub, after_ref, basis_ref, bas_ref, slot_s):
    groups, rho, _ = slot_s.shape
    slots = rho // GROUP

    def body(index, carry):
        x = basis_ref[0, pl.ds(pl.multiple_of(index * sub, sub), sub), :].astype(f32)
        for k in range(slots):
            tile, off = divmod(k * basis_count, 128)
            if off + basis_count <= 128:
                part = x[:, tile * 128 : tile * 128 + 128]
                if off:
                    part = pltpu.roll(part, 128 - off, 1)
            else:
                part = pltpu.roll(x[:, tile * 128 : tile * 128 + 256], 256 - off, 1)[:, :128]
            for g in range(groups):
                slot_s[g, k * GROUP : (k + 1) * GROUP, :] = part[g * GROUP : (g + 1) * GROUP, :]
        for g in range(groups):
            first = pl.multiple_of((index * groups + g) * rho, rho)
            bas_ref[pl.ds(first, rho), :] = slot_s[g].astype(bf16)
        return carry

    lax.fori_loop(0, basis_ref.shape[1] // sub, body, 0)


def align(triplet_basis, basis_count, slots, after):
    _, edges, wide = triplet_basis.shape
    rho = slots * GROUP
    padded = 128
    block = 128
    sub = 64
    return pl.pallas_call(
        functools.partial(align_kernel, basis_count, sub),
        grid=(edges // block,),
        out_shape=jax.ShapeDtypeStruct((edges * slots, padded), bf16),
        in_specs=[
            pl.BlockSpec(memory_space=pl.ANY),
            pl.BlockSpec((1, block, wide), lambda i: (0, i, 0)),
        ],
        out_specs=pl.BlockSpec((block * slots, padded), lambda i: (i, 0)),
        scratch_shapes=[pltpu.VMEM((sub // GROUP, rho, padded), f32)],
        compiler_params=params(),
        cost_estimate=pl.CostEstimate(
            flops=0, transcendentals=0, bytes_accessed=edges * slots * padded * 10
        ),
        name="align",
    )(after, triplet_basis)


def forward_kernel(sub, lists, bas_ref, trip_ref, red_ref, wb_ref, *rest):
    recv_refs = rest[:lists]
    outer_ref, state_ref, pool, wide, gat_s, num_s = rest[lists:]
    narrow, edges = red_ref.shape
    capacity = recv_refs[0].shape[1]
    rho = trip_ref.shape[1]
    padded = bas_ref.shape[1]
    locals_ = edges // capacity

    @pl.when(pl.program_id(0) == 0)
    def _():
        for h in range(locals_):
            pool[h * narrow : (h + 1) * narrow, :] = red_ref[:, h * capacity : (h + 1) * capacity]
        for h in range(lists):
            pool[(locals_ + h) * narrow : (locals_ + h + 1) * narrow, :] = recv_refs[h][...]
        widen_weights(wb_ref, wide)
        num_s[...] = low_iota(capacity, rho)

    groups = sub // GROUP
    own = iota((GROUP, rho), 1) % GROUP == iota((GROUP, rho), 0)

    def body(index, carry):
        first = pl.multiple_of(index * sub, sub)
        first_group = pl.multiple_of(index * groups, groups)

        def gather(g):
            low, high = split_index(trip_ref[pl.ds(first_group + g, 1), :], capacity)
            found = mm(pool[...], low_hot(low, num_s[...]))
            gathered = jnp.zeros((narrow, rho), f32)
            for h in range(locals_ + lists):
                gathered = jnp.where(high == h, found[h * narrow : (h + 1) * narrow, :], gathered)
            gat_s[g] = gathered

        def product(g):
            spread = jnp.concatenate(
                [
                    jnp.where(own, gat_s[g, pl.ds(c, GROUP, stride=0), :], 0.0)
                    for c in range(narrow)
                ],
                axis=0,
            ).astype(bf16)
            bas = bas_ref[pl.ds(pl.multiple_of((first_group + g) * rho, rho), rho), :]
            return mm(spread, bas)

        gather(0)
        held = None
        for g in range(groups):
            if g + 1 < groups:
                gather(g + 1)
            outer = product(g)
            if g % 2 == 0:
                held = outer
                continue
            rows = pl.ds(pl.multiple_of(first + (g - 1) * GROUP, 2 * GROUP), 2 * GROUP)
            for c in range(narrow):
                part = slice(c * GROUP, (c + 1) * GROUP)
                outer_ref[rows, c * padded : (c + 1) * padded] = jnp.concatenate(
                    [held[part, :], outer[part, :]], axis=0
                ).astype(bf16)
        return carry

    lax.fori_loop(0, outer_ref.shape[0] // sub, body, 0)
    state_ref[...] = mm(outer_ref[...], wide[...]).astype(bf16)


def forward(bas, trips, red, recv, w_bil):
    narrow, edges = red.shape
    lists = len(recv)
    capacity = recv[0].shape[1]
    rho = trips.shape[1]
    padded = bas.shape[1]
    block = 256
    sub = 64
    resident = lambda *shape: pl.BlockSpec(shape, lambda i: (0,) * len(shape))
    return pl.pallas_call(
        functools.partial(forward_kernel, sub, lists),
        grid=(edges // block,),
        out_shape=(
            jax.ShapeDtypeStruct((edges, narrow * padded), bf16),
            jax.ShapeDtypeStruct((edges, narrow), bf16),
        ),
        in_specs=[
            pl.BlockSpec((block * rho // GROUP, padded), lambda i: (i, 0)),
            pl.BlockSpec((block // GROUP, rho), lambda i: (i, 0)),
            resident(narrow, edges),
            resident(*w_bil.shape),
        ]
        + [resident(narrow, capacity)] * lists,
        out_specs=(
            pl.BlockSpec((block, narrow * padded), lambda i: (i, 0)),
            pl.BlockSpec((block, narrow), lambda i: (i, 0)),
        ),
        scratch_shapes=[
            pltpu.VMEM((edges // capacity * narrow + lists * narrow, capacity), bf16),
            pltpu.VMEM((narrow * padded, narrow), bf16),
            pltpu.VMEM((sub // GROUP, narrow, rho), f32),
            pltpu.VMEM((capacity, rho), bf16),
        ],
        compiler_params=params(),
        name="forward",
    )(bas, trips, red, w_bil, *recv)


def settle(core_ref, keep_ref, give_ref, pair, part, even, odd):
    is_odd = core_ref[0, 0] == 1
    keep_ref[pair, :, part] = jnp.where(is_odd, odd, even).astype(bf16)
    give_ref[pair, :, part] = jnp.where(is_odd, even, odd).astype(bf16)


def state_kernel(
    scale, parts, lists,
    count_ref, core_ref, outer_ref, state_ref, cot_ref, rev_ref, own_ref, wu_ref, *rest
):
    recv_refs = rest[:lists]
    grad_ref, keep_ref, give_ref, ca_s, ac_s, bil_s = rest[lists:]
    block, narrow = state_ref.shape
    edges = own_ref.shape[1]
    capacity, model = recv_refs[0].shape
    columns = outer_ref.shape[1]
    pid = pl.program_id(0)

    @pl.when(pid == 0)
    def _():
        ca_s[...] = jnp.zeros_like(ca_s)
        ac_s[...] = jnp.zeros_like(ac_s)
        bil_s[...] = jnp.zeros_like(bil_s)

    state = state_ref[...]
    alive = pid * block + iota((block, 1), 0) < count_ref[0, 0]
    scaled = jnp.where(alive, cot_ref[0].astype(f32) * inv_root, 0.0)
    pre_ca = mm(state, wu_ref[0])
    grad_ca = (scaled * silu_slope(pre_ca)).astype(bf16)
    reverse = rev_ref[...]
    mirror = mm(one_hot(reverse, (edges, block), 0), own_ref[0], TN)
    for which, recv_ref in enumerate(recv_refs):
        base = edges + which * capacity
        mirror = mirror + mm(one_hot(reverse - base, (capacity, block), 0), recv_ref[...], TN)
    pre_ac = mm(state, wu_ref[1])
    grad_ac = (mirror * inv_root * silu_slope(pre_ac)).astype(bf16)
    ca_s[...] += mm(grad_ca, state, TN)
    ac_s[...] += mm(grad_ac, state, TN)
    back_rev = mm(grad_ac, wu_ref[1], NT).astype(bf16).astype(f32)
    grad_state = (mm(grad_ca, wu_ref[0], NT) + back_rev).astype(bf16)
    grad_ref[...] = grad_state
    wide_step = 1024
    for start in range(0, columns, wide_step):
        bil_s[:, start : start + wide_step] += mm(
            grad_state, outer_ref[:, start : start + wide_step], TN
        )

    @pl.when(pid == pl.num_programs(0) - 1)
    def _():
        span = columns // parts
        thin = model // parts
        both = jnp.concatenate([ca_s[...], ac_s[...]], axis=1)
        if thin < narrow:
            spare = jnp.zeros((narrow - thin, 2 * narrow), f32)
        for pair in range(parts // 2):
            even = slice(2 * pair * span, (2 * pair + 1) * span)
            odd = slice((2 * pair + 1) * span, (2 * pair + 2) * span)
            settle(core_ref, keep_ref, give_ref, pair, slice(0, span),
                   bil_s[:, even] * scale, bil_s[:, odd] * scale)
            sides = []
            for dest in (2 * pair, 2 * pair + 1):
                piece = both[dest * thin : (dest + 1) * thin, :] * scale
                if thin < narrow:
                    piece = jnp.concatenate([piece, spare], axis=0)
                sides.append(piece)
            settle(core_ref, keep_ref, give_ref, pair, slice(span, span + 2 * narrow), *sides)


def state_grads(count, core, outer, state, cotangent, rev, recv_cot, w_up, scale, parts):
    edges, narrow = state.shape
    model = cotangent.shape[2]
    columns = outer.shape[1]
    block = 256
    lists = len(recv_cot)
    share = (parts // 2, narrow, columns // parts + 2 * narrow)
    resident = lambda *shape: pl.BlockSpec(shape, lambda i: (0,) * len(shape))
    return pl.pallas_call(
        functools.partial(state_kernel, scale, parts, lists),
        grid=(edges // block,),
        out_shape=(
            jax.ShapeDtypeStruct((edges, narrow), bf16),
            jax.ShapeDtypeStruct(share, bf16),
            jax.ShapeDtypeStruct(share, bf16),
        ),
        in_specs=[
            smem(),
            smem(),
            pl.BlockSpec((block, columns), lambda i: (i, 0)),
            pl.BlockSpec((block, narrow), lambda i: (i, 0)),
            pl.BlockSpec((1, block, model), lambda i: (0, i, 0)),
            pl.BlockSpec((1, block), lambda i: (0, i)),
            resident(1, edges, model),
            resident(*w_up.shape),
        ]
        + [resident(*recv_cot[0].shape)] * lists,
        out_specs=(
            pl.BlockSpec((block, narrow), lambda i: (i, 0)),
            resident(*share),
            resident(*share),
        ),
        scratch_shapes=[
            pltpu.VMEM((model, narrow), f32),
            pltpu.VMEM((model, narrow), f32),
            pltpu.VMEM((narrow, columns), f32),
        ],
        compiler_params=params(),
        name="state_grads",
    )(count, core, outer, state, cotangent, rev, cotangent, w_up, *recv_cot)


def own_rows(mixed, narrow):
    rho = mixed.shape[1]
    value = mixed.reshape(narrow // GROUP, GROUP, GROUP, rho)
    shape = (1, 1, GROUP, rho)
    row, lane = iota(shape, 2), iota(shape, 3)
    step = GROUP // 2
    while step:
        low, high = value[:, :step], value[:, step:]
        upper = jnp.bitwise_and(row, step) > 0
        kept = jnp.bitwise_and(row, step) == jnp.bitwise_and(lane, step)
        straight = jnp.where(upper, high, low)
        other = jnp.where(upper, low, high)
        moved = pltpu.roll(other, step, 2)
        if 2 * step != GROUP:
            moved = jnp.where(upper, moved, pltpu.roll(other, GROUP - step, 2))
        value = jnp.where(kept, straight, moved)
        step //= 2
    return value.reshape(narrow, rho)


def backward_kernel(sub, lists, bas_ref, grad_ref, trip_ref, wb_ref, home_ref, *rest):
    back_refs = rest[:lists]
    pool_s, wide, turn_s, cast_s, hot_s, num_s = rest[lists:]
    block, narrow = grad_ref.shape
    padded = bas_ref.shape[1]
    rho = trip_ref.shape[1]
    rows, capacity = pool_s.shape
    pid = pl.program_id(0)

    @pl.when(pid == 0)
    def _():
        widen_weights(wb_ref, wide)
        pool_s[...] = jnp.zeros_like(pool_s)
        num_s[...] = low_iota(capacity, rho)

    grad_state = grad_ref[...]
    height = narrow * GROUP

    def spread(pair, carry):
        start = pl.multiple_of(pair * 2 * padded, 2 * padded)
        grad = mm(grad_state, wide[pl.ds(start, 2 * padded), :], NT)
        for g in range(block // GROUP):
            for side in range(2):
                at = pl.multiple_of(g * height + pair * 2 * GROUP + side * GROUP, GROUP)
                turn_s[pl.ds(at, GROUP), :] = grad[
                    g * GROUP : (g + 1) * GROUP, side * padded : (side + 1) * padded
                ]
        return carry

    lax.fori_loop(0, narrow // 2, spread, 0, unroll=4)
    groups = sub // GROUP

    def body(index, carry):
        first_group = pl.multiple_of(index * groups, groups)

        def mix(g):
            here = first_group + g
            bas = bas_ref[pl.ds(pl.multiple_of(here * rho, rho), rho), :]
            grads = turn_s[pl.ds(pl.multiple_of(here * height, height), height), :]
            return mm(grads.astype(bf16), bas, NT)

        def cast(g, mixed):
            trip_grad = own_rows(mixed, narrow).astype(bf16)
            low, high = split_index(trip_ref[pl.ds(first_group + g, 1), :], capacity)
            part = slice(g * rho, (g + 1) * rho)
            hot_s[:, part] = low_hot(low, num_s[...])
            zero = jnp.zeros_like(trip_grad)
            wide_high = jnp.broadcast_to(high.astype(f32).astype(bf16), trip_grad.shape)
            for h in range(rows // narrow):
                cast_s[h * narrow : (h + 1) * narrow, part] = jnp.where(
                    wide_high == jnp.asarray(h, bf16), trip_grad, zero
                )

        ready = mix(0)
        for g in range(groups):
            mixed = ready
            if g + 1 < groups:
                ready = mix(g + 1)
            cast(g, mixed)
        pool_s[...] += mm(cast_s[...], hot_s[...], NT)
        return carry

    lax.fori_loop(0, block // sub, body, 0)

    @pl.when(pid == pl.num_programs(0) - 1)
    def _():
        home = home_ref.shape[0]
        home_ref[...] = pool_s[:home, :]
        for which, back_ref in enumerate(back_refs):
            first = home + which * narrow
            back_ref[...] = pool_s[first : first + narrow, :].astype(bf16)


def backward(bas, grad_state, trips, w_bil, capacity, lists):
    edges, narrow = grad_state.shape
    rho = trips.shape[1]
    padded = bas.shape[1]
    block = 256
    sub = 64
    home = edges // capacity * narrow
    rows = home + lists * narrow
    resident = lambda *shape: pl.BlockSpec(shape, lambda i: (0,) * len(shape))
    return pl.pallas_call(
        functools.partial(backward_kernel, sub, lists),
        grid=(edges // block,),
        out_shape=(jax.ShapeDtypeStruct((home, capacity), f32),)
        + (jax.ShapeDtypeStruct((narrow, capacity), bf16),) * lists,
        in_specs=[
            pl.BlockSpec((block * rho // GROUP, padded), lambda i: (i, 0)),
            pl.BlockSpec((block, narrow), lambda i: (i, 0)),
            pl.BlockSpec((block // GROUP, rho), lambda i: (i, 0)),
            resident(*w_bil.shape),
        ],
        out_specs=(resident(home, capacity),) + (resident(narrow, capacity),) * lists,
        scratch_shapes=[
            pltpu.VMEM((rows, capacity), f32),
            pltpu.VMEM((narrow * padded, narrow), bf16),
            pltpu.VMEM((block * narrow, padded), f32),
            pltpu.VMEM((rows, sub // GROUP * rho), bf16),
            pltpu.VMEM((capacity, sub // GROUP * rho), bf16),
            pltpu.VMEM((capacity, rho), bf16),
        ],
        compiler_params=params(),
        name="backward",
    )(bas, grad_state, trips, w_bil)


def tail_kernel(
    scale, parts, lists,
    count_ref, core_ref, pool_ref, rows_ref, pdt_ref, pre_ref, hid_ref, x_ref, we_ref, wd_ref, *rest
):
    back_refs = rest[:lists]
    out_ref, keep_ref, give_ref, grad_s = rest[lists:]
    narrow, edges = pdt_ref.shape
    capacity = back_refs[0].shape[1]
    model = pre_ref.shape[1]
    grad = jnp.concatenate(
        [pool_ref[h * narrow : (h + 1) * narrow, :] for h in range(edges // capacity)], axis=1
    )
    for which, back_ref in enumerate(back_refs):
        grad = grad + mm(back_ref[...], send_hot(rows_ref, count_ref, which, edges), NT)
    grad_down = (grad * silu_slope(pdt_ref[...])).astype(bf16)
    step = 256
    for start in range(0, edges, step):
        part = slice(start, start + step)
        grad_hidden = lax.dot_general(
            grad_down[:, part], wd_ref[...], (((0,), (1,)), ((), ())), preferred_element_type=f32
        )
        grad_edge = (grad_hidden * silu_slope(pre_ref[part, :])).astype(bf16)
        grad_s[part, :] = grad_edge
        out_ref[0, part, :] = mm(grad_edge, we_ref[...], NT).astype(bf16)
    down = lax.dot_general(
        hid_ref[...], grad_down, (((0,), (1,)), ((), ())), preferred_element_type=f32
    )
    down = jnp.concatenate([down, jnp.zeros_like(down)], axis=1)
    span = model // parts
    for start in range(0, model, step):
        edge = mm(x_ref[0, :, start : start + step], grad_s[...], TN)
        both = jnp.concatenate([edge, down[start : start + step, :]], axis=1) * scale
        for first in range(0, step, 2 * span):
            settle(
                core_ref, keep_ref, give_ref, (start + first) // (2 * span), slice(None),
                both[first : first + span, :], both[first + span : first + 2 * span, :],
            )


def tail(pool, back, rows, counts, core, pdt, pre, hidden, messages, w_edge, w_down, scale, parts):
    _, edges, model = messages.shape
    narrow = w_down.shape[1]
    share = jax.ShapeDtypeStruct((parts // 2, model // parts, model + 2 * narrow), bf16)
    return pl.pallas_call(
        functools.partial(tail_kernel, scale, parts, len(back)),
        out_shape=(
            jax.ShapeDtypeStruct((1, edges, model), bf16),
            share,
            share,
        ),
        in_specs=[smem(), smem()] + [vmem()] * (8 + len(back)),
        out_specs=(vmem(),) * 3,
        scratch_shapes=[pltpu.VMEM((edges, model), bf16)],
        compiler_params=params(),
        name="tail",
    )(counts, core, pool, rows, pdt, pre, hidden, messages, w_edge, w_down, *back)


def add_pair_kernel(chip_ref, keep_ref, got_ref, mine_ref, *out_refs):
    chips = keep_ref.shape[0]
    chip = chip_ref[0, 0]
    for step, out_ref in enumerate((mine_ref,) + out_refs):
        at = lax.rem(chip + step, chips)
        out_ref[...] = (keep_ref[at].astype(f32) + got_ref[at].astype(f32)).astype(bf16)


def add_kernel(*refs):
    *in_refs, out_ref = refs
    total = in_refs[0][...].astype(f32)
    for in_ref in in_refs[1:]:
        total = total + in_ref[...].astype(f32)
    out_ref[...] = total.astype(bf16)


def over_graph(keep, give, chip):
    chips, height, wide = keep.shape
    devices = 2 * chips
    piece = jax.ShapeDtypeStruct((height, wide), bf16)
    got = lax.ppermute(give, "graph", [(i, i ^ 1) for i in range(devices)])
    mine, *sends = pl.pallas_call(
        add_pair_kernel,
        out_shape=(piece,) * chips,
        in_specs=[smem(), vmem(), vmem()],
        out_specs=(vmem(),) * chips,
        compiler_params=params(),
    )(chip, keep, got)
    arrived = []
    for step, send in enumerate(sends):
        route = [(i, (i + 2 * (step + 1)) % devices) for i in range(devices)]
        arrived.append(lax.ppermute(send, "graph", route))
    return pl.pallas_call(
        add_kernel,
        out_shape=piece,
        in_specs=[vmem()] * chips,
        out_specs=vmem(),
        compiler_params=params(),
    )(mine, *arrived)


def over_dp(share):
    slabs = lax.axis_size("dp")
    copies = [share]
    for step in range(1, slabs):
        copies.append(lax.ppermute(share, "dp", [(i, i ^ step) for i in range(slabs)]))
    return copies


def paired_sum(values):
    while len(values) > 1:
        values = [values[i] + values[i + 1] for i in range(0, len(values), 2)]
    return values[0]


def finish_kernel(slabs, *refs):
    early_refs, late_refs = refs[:slabs], refs[slabs : 2 * slabs]
    edge_ref, down_ref, bil_ref, up_ref = refs[2 * slabs :]
    rows, model = edge_ref.shape
    basis = bil_ref.shape[0]
    _, narrow, _ = up_ref.shape
    padded = 128
    span = bil_ref.shape[1] // narrow * padded

    def total(in_refs, *part):
        return paired_sum([in_ref[part].astype(f32) for in_ref in in_refs])

    every = slice(None)
    for c in range(bil_ref.shape[1] // narrow):
        block = total(early_refs, every, slice(c * padded, (c + 1) * padded))
        bil_ref[:, c * narrow : (c + 1) * narrow] = block.T[:basis, :]
    both = total(early_refs, slice(0, rows), slice(span, span + 2 * narrow)).T
    up_ref[0] = both[:narrow, :]
    up_ref[1] = both[narrow:, :]
    edge_ref[...] = total(late_refs, every, slice(0, model))
    down_ref[...] = total(late_refs, every, slice(model, model + 2 * narrow))[:, :narrow]


def finish(early, late, basis, narrow, model, parts):
    rows = model // parts
    return pl.pallas_call(
        functools.partial(finish_kernel, len(early)),
        out_shape=(
            jax.ShapeDtypeStruct((rows, model), f32),
            jax.ShapeDtypeStruct((rows, narrow), f32),
            jax.ShapeDtypeStruct((basis, narrow * narrow // parts), f32),
            jax.ShapeDtypeStruct((2, narrow, rows), f32),
        ),
        in_specs=[vmem()] * (len(early) + len(late)),
        out_specs=(vmem(),) * 4,
        compiler_params=params(),
        name="finish",
    )(*early, *late)


def body(
    messages,
    cotangent,
    triplet_basis,
    w_edge,
    w_down,
    w_bil,
    w_up,
    trip_src,
    send_rows,
    send_count,
    rev_src,
    edge_count,
):
    _, edges, model = messages.shape
    narrow = w_down.shape[1]
    slots = trip_src.shape[2]
    _, lists, capacity = send_rows.shape
    basis_count = w_bil.shape[0]
    parts = lax.axis_size("graph")
    scale = 1.0 / math.sqrt(lax.axis_size("dp") * parts * edges)
    shifts = offsets(lists)
    place = lax.axis_index("graph").reshape(1, 1)
    core, chip = place % 2, place // 2
    trips = (
        trip_src[0]
        .reshape(edges // GROUP, GROUP, slots)
        .transpose(0, 2, 1)
        .reshape(edges // GROUP, GROUP * slots)
    )

    def exchange(blocks, sign):
        moved = []
        for which in range(lists):
            moved.append(shifted(blocks[which], "graph", sign * shifts[which]))
        return moved

    pre, hidden, pdt, red, *send_red = front(messages, w_edge, w_down, send_rows, send_count)
    recv_red = exchange(send_red, 1)
    send_cot = pick(cotangent, send_rows, send_count, red)
    recv_cot = exchange(send_cot, 1)
    bas = align(triplet_basis, basis_count, slots, send_cot[0])
    outer, state = forward(bas, trips, red, recv_red, w_bil)
    grad_state, keep, give = state_grads(
        edge_count, core, outer, state, cotangent, rev_src, recv_cot, w_up, scale, parts
    )
    early = over_graph(keep, give, chip)
    home, *returned = backward(bas, grad_state, trips, w_bil, capacity, lists)
    back = exchange(returned, -1)
    early = over_dp(early)
    grad_messages, keep, give = tail(
        home, back, send_rows, send_count, core, pdt, pre, hidden, messages, w_edge, w_down,
        scale, parts,
    )
    late = over_dp(over_graph(keep, give, chip))
    edge_out, down_out, bil_out, up_out = finish(early, late, basis_count, narrow, model, parts)
    return (grad_messages, edge_out, down_out, bil_out, up_out)


def solution(mesh):
    return jax.shard_map(
        body,
        mesh=mesh,
        in_specs=(
            P("dp", "graph", None),
            P("dp", "graph", None),
            P("dp", "graph", None),
            P(),
            P(),
            P(),
            P(),
            P("dp", "graph", None),
            P("dp", "graph", None),
            P("dp", "graph"),
            P("dp", "graph"),
            P("dp", "graph"),
        ),
        out_specs=(
            P("dp", "graph", None),
            P("graph", None),
            P("graph", None),
            P(None, "graph"),
            P(None, None, "graph"),
        ),
        check_vma=False,
    )
```

```python
import functools
import math

import jax
import jax.numpy as jnp
from jax import lax
from jax.experimental import pallas as pl
from jax.experimental.pallas import tpu as pltpu
from jax.sharding import PartitionSpec as P


inv_root = 0.7071067811865476
bf16 = jnp.bfloat16
f32 = jnp.float32
GROUP = 8
NN = (((1,), (0,)), ((), ()))
NT = (((1,), (1,)), ((), ()))
TN = (((0,), (0,)), ((), ()))


def mm(left, right, dims=NN):
    return lax.dot_general(left, right, dims, preferred_element_type=f32)


def silu_slope(values):
    sigma = jax.nn.sigmoid(values)
    return sigma * (1.0 + values * (1.0 - sigma))


def offsets(count):
    return [(which // 2 + 1) * (1 - 2 * (which % 2)) for which in range(count)]


def shifted(block, axis, distance):
    devices = range(lax.axis_size(axis))
    route = [((i - distance) % len(devices), i) for i in devices]
    return lax.ppermute(block, axis, route)


def iota(shape, dim):
    return lax.broadcasted_iota(jnp.int32, shape, dim)


def one_hot(index, shape, dim):
    return jnp.where(index == iota(shape, dim), 1.0, 0.0).astype(bf16)


def vmem():
    return pl.BlockSpec(memory_space=pltpu.VMEM)


def params(mib=12):
    return pltpu.CompilerParams(vmem_limit_bytes=mib * 1024 * 1024)


def cost(edges, weight):
    return pl.CostEstimate(
        flops=weight * edges * 10**6, transcendentals=0, bytes_accessed=weight * edges * 1000
    )


def send_hot(rows_ref, count_ref, which, edges):
    capacity = rows_ref.shape[2]
    rows = rows_ref[0, which : which + 1, :]
    used = iota((1, capacity), 1) < count_ref[0, which]
    return one_hot(jnp.where(used, rows, -1), (edges, capacity), 0)


def front_kernel(
    count_ref, x_ref, we_ref, wd_ref, rows_ref, pre_ref, hid_ref, pdt_ref, red_ref, *send_refs
):
    edges = x_ref.shape[1]
    step = 256
    for start in range(0, edges, step):
        pre = mm(x_ref[0, start : start + step, :], we_ref[...])
        pre_ref[start : start + step, :] = pre
        hidden = (pre * jax.nn.sigmoid(pre)).astype(bf16)
        hid_ref[start : start + step, :] = hidden
        down = mm(wd_ref[...], hidden, NT)
        pdt_ref[:, start : start + step] = down
        red_ref[:, start : start + step] = (down * jax.nn.sigmoid(down)).astype(bf16)
    for which, send_ref in enumerate(send_refs):
        hot = send_hot(rows_ref, count_ref, which, edges)
        send_ref[...] = mm(red_ref[...], hot).astype(bf16)


def smem():
    return pl.BlockSpec(memory_space=pltpu.SMEM)


def front(messages, w_edge, w_down, rows, counts):
    _, edges, model = messages.shape
    narrow = w_down.shape[0]
    _, lists, capacity = rows.shape
    return pl.pallas_call(
        front_kernel,
        out_shape=(
            jax.ShapeDtypeStruct((edges, model), f32),
            jax.ShapeDtypeStruct((edges, model), bf16),
            jax.ShapeDtypeStruct((narrow, edges), f32),
            jax.ShapeDtypeStruct((narrow, edges), bf16),
        )
        + (jax.ShapeDtypeStruct((narrow, capacity), bf16),) * lists,
        in_specs=[smem()] + [vmem()] * 4,
        out_specs=(vmem(),) * (4 + lists),
        compiler_params=params(),
        cost_estimate=cost(edges, 3),
        name="front",
    )(counts, messages, w_edge, w_down, rows)


def pick_kernel(count_ref, cot_ref, rows_ref, trip_ref, after_ref, low_ref, high_ref, *send_refs):
    edges = cot_ref.shape[1]
    capacity = rows_ref.shape[2]
    groups, rho = low_ref.shape
    slots = rho // GROUP
    trip = trip_ref[0]
    repeat = one_hot(iota((slots, rho), 1) // GROUP, (slots, rho), 0)
    own = iota((edges, rho), 0) % GROUP == iota((edges, rho), 1) % GROUP
    gather = one_hot(iota((groups, edges), 1) // GROUP, (groups, edges), 0)

    def slot_major(values):
        spread = mm(values.astype(f32).astype(bf16), repeat)
        return mm(gather, jnp.where(own, spread, 0.0).astype(bf16))

    low_ref[...] = slot_major(jnp.bitwise_and(trip, capacity - 1))
    high_ref[...] = slot_major(jnp.right_shift(trip, capacity.bit_length() - 1)).astype(jnp.int32)
    for which, send_ref in enumerate(send_refs):
        hot = send_hot(rows_ref, count_ref, which, edges)
        send_ref[...] = mm(hot, cot_ref[0], TN).astype(bf16)


def pick(cotangent, rows, counts, trips, after):
    _, edges, model = cotangent.shape
    _, lists, capacity = rows.shape
    slot_major = (edges // GROUP, trips.shape[2] * GROUP)
    return pl.pallas_call(
        pick_kernel,
        out_shape=(
            jax.ShapeDtypeStruct(slot_major, f32),
            jax.ShapeDtypeStruct(slot_major, jnp.int32),
        )
        + (jax.ShapeDtypeStruct((capacity, model), bf16),) * lists,
        in_specs=[smem(), vmem(), vmem(), vmem(), pl.BlockSpec(memory_space=pl.ANY)],
        out_specs=(vmem(),) * (2 + lists),
        compiler_params=params(),
        cost_estimate=cost(edges, 3),
        name="pick",
    )(counts, cotangent, rows, trips, after)


def widen_weights(wb_ref, wide):
    basis, _ = wb_ref.shape
    narrow = wide.shape[1]
    padded = wide.shape[0] // narrow
    zeros = jnp.zeros((padded - basis, narrow), bf16)
    for c in range(0, narrow, 2):
        pair = wb_ref[:, c * narrow : (c + 2) * narrow]
        wide[c * padded : (c + 1) * padded, :] = jnp.concatenate(
            [pair[:, :narrow], zeros], axis=0
        )
        wide[(c + 1) * padded : (c + 2) * padded, :] = jnp.concatenate(
            [pair[:, narrow:], zeros], axis=0
        )


def low_iota(capacity, rho):
    return iota((capacity, rho), 0).astype(f32).astype(bf16)


def low_hot(low, numbers):
    one, zero = jnp.ones((), bf16), jnp.zeros((), bf16)
    return jnp.where(low == numbers, one, zero)


def align_kernel(basis_count, sub, after_ref, basis_ref, bas_ref, slot_s):
    groups, rho, _ = slot_s.shape
    slots = rho // GROUP

    def body(index, carry):
        x = basis_ref[0, pl.ds(pl.multiple_of(index * sub, sub), sub), :].astype(f32)
        for k in range(slots):
            tile, off = divmod(k * basis_count, 128)
            if off + basis_count <= 128:
                part = x[:, tile * 128 : tile * 128 + 128]
                if off:
                    part = pltpu.roll(part, 128 - off, 1)
            else:
                part = pltpu.roll(x[:, tile * 128 : tile * 128 + 256], 256 - off, 1)[:, :128]
            for g in range(groups):
                slot_s[g, k * GROUP : (k + 1) * GROUP, :] = part[g * GROUP : (g + 1) * GROUP, :]
        for g in range(groups):
            first = pl.multiple_of((index * groups + g) * rho, rho)
            bas_ref[pl.ds(first, rho), :] = slot_s[g].astype(bf16)
        return carry

    lax.fori_loop(0, basis_ref.shape[1] // sub, body, 0)


def align(triplet_basis, basis_count, slots, after):
    _, edges, wide = triplet_basis.shape
    rho = slots * GROUP
    padded = 128
    block = 128
    sub = 64
    return pl.pallas_call(
        functools.partial(align_kernel, basis_count, sub),
        grid=(edges // block,),
        out_shape=jax.ShapeDtypeStruct((edges * slots, padded), bf16),
        in_specs=[
            pl.BlockSpec(memory_space=pl.ANY),
            pl.BlockSpec((1, block, wide), lambda i: (0, i, 0)),
        ],
        out_specs=pl.BlockSpec((block * slots, padded), lambda i: (i, 0)),
        scratch_shapes=[pltpu.VMEM((sub // GROUP, rho, padded), f32)],
        compiler_params=params(12),
        cost_estimate=cost(edges, 6),
        name="align",
    )(after, triplet_basis)


def forward_kernel(sub, lists, bas_ref, low_ref, high_ref, red_ref, wb_ref, *rest):
    recv_refs = rest[:lists]
    outer_ref, state_ref, wide, pool, gat_s, num_s = rest[lists:]
    narrow, edges = red_ref.shape
    capacity = recv_refs[0].shape[1]
    rho = low_ref.shape[1]
    padded = bas_ref.shape[1]
    locals_ = edges // capacity

    @pl.when(pl.program_id(0) == 0)
    def _():
        for h in range(locals_):
            pool[h * narrow : (h + 1) * narrow, :] = red_ref[:, h * capacity : (h + 1) * capacity]
        for h in range(lists):
            pool[(locals_ + h) * narrow : (locals_ + h + 1) * narrow, :] = recv_refs[h][...]
        widen_weights(wb_ref, wide)
        num_s[...] = low_iota(capacity, rho)

    groups = sub // GROUP
    own = iota((GROUP, rho), 1) % GROUP == iota((GROUP, rho), 0)

    def body(index, carry):
        first = pl.multiple_of(index * sub, sub)
        first_group = pl.multiple_of(index * groups, groups)

        def gather(g):
            low = low_ref[pl.ds(first_group + g, 1), :].astype(bf16)
            high = high_ref[pl.ds(first_group + g, 1), :]
            found = mm(pool[...], low_hot(low, num_s[...]))
            gathered = jnp.zeros((narrow, rho), f32)
            for h in range(locals_ + lists):
                gathered = jnp.where(high == h, found[h * narrow : (h + 1) * narrow, :], gathered)
            gat_s[g] = gathered

        def product(g):
            spread = jnp.concatenate(
                [
                    jnp.where(own, gat_s[g, pl.ds(c, GROUP, stride=0), :], 0.0)
                    for c in range(narrow)
                ],
                axis=0,
            ).astype(bf16)
            bas = bas_ref[pl.ds(pl.multiple_of((first_group + g) * rho, rho), rho), :]
            return mm(spread, bas)

        gather(0)
        held = None
        for g in range(groups):
            if g + 1 < groups:
                gather(g + 1)
            outer = product(g)
            if g % 2 == 0:
                held = outer
                continue
            rows = pl.ds(pl.multiple_of(first + (g - 1) * GROUP, 2 * GROUP), 2 * GROUP)
            for c in range(narrow):
                part = slice(c * GROUP, (c + 1) * GROUP)
                outer_ref[rows, c * padded : (c + 1) * padded] = jnp.concatenate(
                    [held[part, :], outer[part, :]], axis=0
                ).astype(bf16)
        return carry

    lax.fori_loop(0, outer_ref.shape[0] // sub, body, 0)
    state_ref[...] = mm(outer_ref[...], wide[...]).astype(bf16)


def forward(bas, low, high, red, recv, w_bil):
    narrow, edges = red.shape
    lists = len(recv)
    capacity = recv[0].shape[1]
    rho = low.shape[1]
    padded = bas.shape[1]
    block = 256
    sub = 64
    resident = lambda *shape: pl.BlockSpec(shape, lambda i: (0,) * len(shape))
    return pl.pallas_call(
        functools.partial(forward_kernel, sub, lists),
        grid=(edges // block,),
        out_shape=(
            jax.ShapeDtypeStruct((edges, narrow * padded), bf16),
            jax.ShapeDtypeStruct((edges, narrow), bf16),
            jax.ShapeDtypeStruct((narrow * padded, narrow), bf16),
        ),
        in_specs=[
            pl.BlockSpec((block * rho // GROUP, padded), lambda i: (i, 0)),
            pl.BlockSpec((block // GROUP, rho), lambda i: (i, 0)),
            pl.BlockSpec((block // GROUP, rho), lambda i: (i, 0)),
            resident(narrow, edges),
            resident(*w_bil.shape),
        ]
        + [resident(narrow, capacity)] * lists,
        out_specs=(
            pl.BlockSpec((block, narrow * padded), lambda i: (i, 0)),
            pl.BlockSpec((block, narrow), lambda i: (i, 0)),
            resident(narrow * padded, narrow),
        ),
        scratch_shapes=[
            pltpu.VMEM((edges // capacity * narrow + lists * narrow, capacity), bf16),
            pltpu.VMEM((sub // GROUP, narrow, rho), f32),
            pltpu.VMEM((capacity, rho), bf16),
        ],
        compiler_params=params(32),
        cost_estimate=cost(edges, 29),
        name="forward",
    )(bas, low, high, red, w_bil, *recv)


def settle(core_ref, keep_ref, give_ref, pair, part, even, odd):
    is_odd = core_ref[0, 0] == 1
    keep_ref[pair, :, part] = jnp.where(is_odd, odd, even).astype(bf16)
    give_ref[pair, :, part] = jnp.where(is_odd, even, odd).astype(bf16)


def state_kernel(
    lists, count_ref, state_ref, cot_ref, rev_ref, own_ref, wu_ref, *rest
):
    recv_refs = rest[:lists]
    grad_ref, up_ref, mirror_s, cast_s = rest[lists:]
    block, _ = state_ref.shape
    edges = own_ref.shape[1]
    capacity, model = recv_refs[0].shape
    pid = pl.program_id(0)

    @pl.when(pid == 0)
    def _():
        up_ref[...] = jnp.zeros_like(up_ref)

    row = rev_ref[...].astype(f32)
    reverse = jnp.broadcast_to(row, (GROUP, block)).T[:, :1].astype(jnp.int32)
    mirror = mm(one_hot(reverse, (block, edges), 1), own_ref[0])
    for which, recv_ref in enumerate(recv_refs):
        base = edges + which * capacity
        mirror = mirror + mm(one_hot(reverse - base, (block, capacity), 1), recv_ref[...])
    mirror_s[...] = mirror
    step = 64
    for start in range(0, block, step):
        part = slice(start, start + step)
        state = state_ref[part, :]
        alive = pid * block + start + iota((step, 1), 0) < count_ref[0, 0]
        scaled = jnp.where(alive, cot_ref[0, part, :].astype(f32) * inv_root, 0.0)
        cast_s[part, :model] = (scaled * silu_slope(mm(state, wu_ref[0]))).astype(bf16)
        cast_s[part, model:] = (
            mirror_s[part, :] * inv_root * silu_slope(mm(state, wu_ref[1]))
        ).astype(bf16)
    up_ref[...] += mm(state_ref[...], cast_s[...], TN)
    back_rev = mm(cast_s[:, model:], wu_ref[1], NT).astype(bf16).astype(f32)
    grad_ref[...] = (mm(cast_s[:, :model], wu_ref[0], NT) + back_rev).astype(bf16)


def state_grads(count, state, cotangent, rev, recv_cot, w_up):
    edges, narrow = state.shape
    model = cotangent.shape[2]
    block = 256
    lists = len(recv_cot)
    resident = lambda *shape: pl.BlockSpec(shape, lambda i: (0,) * len(shape))
    return pl.pallas_call(
        functools.partial(state_kernel, lists),
        grid=(edges // block,),
        out_shape=(
            jax.ShapeDtypeStruct((edges, narrow), bf16),
            jax.ShapeDtypeStruct((narrow, 2 * model), f32),
        ),
        in_specs=[
            smem(),
            pl.BlockSpec((block, narrow), lambda i: (i, 0)),
            pl.BlockSpec((1, block, model), lambda i: (0, i, 0)),
            pl.BlockSpec((1, block), lambda i: (0, i)),
            resident(1, edges, model),
            resident(*w_up.shape),
        ]
        + [resident(*recv_cot[0].shape)] * lists,
        out_specs=(
            pl.BlockSpec((block, narrow), lambda i: (i, 0)),
            resident(narrow, 2 * model),
        ),
        scratch_shapes=[
            pltpu.VMEM((block, model), f32),
            pltpu.VMEM((block, 2 * model), bf16),
        ],
        compiler_params=params(16),
        cost_estimate=cost(edges, 7),
        name="state_grads",
    )(count, state, cotangent, rev, cotangent, w_up, *recv_cot)


def bil_kernel(scale, parts, core_ref, outer_ref, grad_ref, up_ref, keep_ref, give_ref, bil_s):
    narrow, columns = bil_s.shape
    model = up_ref.shape[1] // 2
    pid = pl.program_id(0)

    @pl.when(pid == 0)
    def _():
        bil_s[...] = jnp.zeros_like(bil_s)

    wide_step = 1024
    for start in range(0, columns, wide_step):
        bil_s[:, start : start + wide_step] += mm(
            grad_ref[...], outer_ref[:, start : start + wide_step], TN
        )

    @pl.when(pid == pl.num_programs(0) - 1)
    def _():
        span = columns // parts
        thin = model // parts
        both = jnp.concatenate([up_ref[:, :model], up_ref[:, model:]], axis=0).T
        if thin < narrow:
            spare = jnp.zeros((narrow - thin, 2 * narrow), f32)
        for pair in range(parts // 2):
            even = slice(2 * pair * span, (2 * pair + 1) * span)
            odd = slice((2 * pair + 1) * span, (2 * pair + 2) * span)
            settle(core_ref, keep_ref, give_ref, pair, slice(0, span),
                   bil_s[:, even] * scale, bil_s[:, odd] * scale)
            sides = []
            for dest in (2 * pair, 2 * pair + 1):
                piece = both[dest * thin : (dest + 1) * thin, :] * scale
                if thin < narrow:
                    piece = jnp.concatenate([piece, spare], axis=0)
                sides.append(piece)
            settle(core_ref, keep_ref, give_ref, pair, slice(span, span + 2 * narrow), *sides)


def bil_shares(core, outer, grad_state, up, scale, parts):
    edges, narrow = grad_state.shape
    columns = outer.shape[1]
    block = 256
    share = (parts // 2, narrow, columns // parts + 2 * narrow)
    resident = lambda *shape: pl.BlockSpec(shape, lambda i: (0,) * len(shape))
    return pl.pallas_call(
        functools.partial(bil_kernel, scale, parts),
        grid=(edges // block,),
        out_shape=(jax.ShapeDtypeStruct(share, bf16),) * 2,
        in_specs=[
            smem(),
            pl.BlockSpec((block, columns), lambda i: (i, 0)),
            pl.BlockSpec((block, narrow), lambda i: (i, 0)),
            resident(*up.shape),
        ],
        out_specs=(resident(*share),) * 2,
        scratch_shapes=[pltpu.VMEM((narrow, columns), f32)],
        compiler_params=params(20),
        cost_estimate=cost(edges, 4),
        name="bil_shares",
    )(core, outer, grad_state, up)


def own_rows(mixed, narrow):
    rho = mixed.shape[1]
    value = mixed.reshape(narrow // GROUP, GROUP, GROUP, rho)
    shape = (1, 1, GROUP, rho)
    row, lane = iota(shape, 2), iota(shape, 3)
    step = GROUP // 2
    while step:
        low, high = value[:, :step], value[:, step:]
        upper = jnp.bitwise_and(row, step) > 0
        kept = jnp.bitwise_and(row, step) == jnp.bitwise_and(lane, step)
        straight = jnp.where(upper, high, low)
        other = jnp.where(upper, low, high)
        moved = pltpu.roll(other, step, 2)
        if 2 * step != GROUP:
            moved = jnp.where(upper, moved, pltpu.roll(other, GROUP - step, 2))
        value = jnp.where(kept, straight, moved)
        step //= 2
    return value.reshape(narrow, rho)


def backward_kernel(sub, lists, bas_ref, grad_ref, low_ref, high_ref, wide, home_ref, *rest):
    back_refs = rest[:lists]
    pool_s, turn_s, cast_s, hot_s, num_s = rest[lists:]
    block, narrow = grad_ref.shape
    padded = bas_ref.shape[1]
    rho = low_ref.shape[1]
    rows, capacity = pool_s.shape
    pid = pl.program_id(0)

    @pl.when(pid == 0)
    def _():
        pool_s[...] = jnp.zeros_like(pool_s)
        num_s[...] = low_iota(capacity, rho)

    grad_state = grad_ref[...]
    height = narrow * GROUP

    def spread(pair, carry):
        start = pl.multiple_of(pair * 2 * padded, 2 * padded)
        grad = mm(grad_state, wide[pl.ds(start, 2 * padded), :], NT)
        for g in range(block // GROUP):
            part = slice(g * GROUP, (g + 1) * GROUP)
            at = pl.multiple_of(g * height + pair * 2 * GROUP, 2 * GROUP)
            turn_s[pl.ds(at, 2 * GROUP), :] = jnp.concatenate(
                [grad[part, :padded], grad[part, padded:]], axis=0
            ).astype(bf16)
        return carry

    lax.fori_loop(0, narrow // 2, spread, 0, unroll=8)
    groups = sub // GROUP

    def body(index, carry):
        first_group = pl.multiple_of(index * groups, groups)

        def mix(g):
            here = first_group + g
            bas = bas_ref[pl.ds(pl.multiple_of(here * rho, rho), rho), :]
            grads = turn_s[pl.ds(pl.multiple_of(here * height, height), height), :]
            return mm(grads, bas, NT)

        def cast(g, mixed):
            trip_grad = own_rows(mixed, narrow).astype(bf16)
            low = low_ref[pl.ds(first_group + g, 1), :].astype(bf16)
            high = high_ref[pl.ds(first_group + g, 1), :]
            part = slice(g * rho, (g + 1) * rho)
            hot_s[:, part] = low_hot(low, num_s[...])
            zero = jnp.zeros_like(trip_grad)
            wide_high = jnp.broadcast_to(high.astype(f32).astype(bf16), trip_grad.shape)
            for h in range(rows // narrow):
                cast_s[h * narrow : (h + 1) * narrow, part] = jnp.where(
                    wide_high == jnp.asarray(h, bf16), trip_grad, zero
                )

        ready = mix(0)
        for g in range(groups):
            mixed = ready
            if g + 1 < groups:
                ready = mix(g + 1)
            cast(g, mixed)
        pool_s[...] += mm(cast_s[...], hot_s[...], NT)
        return carry

    lax.fori_loop(0, block // sub, body, 0)

    @pl.when(pid == pl.num_programs(0) - 1)
    def _():
        home = home_ref.shape[0]
        home_ref[...] = pool_s[:home, :]
        for which, back_ref in enumerate(back_refs):
            first = home + which * narrow
            back_ref[...] = pool_s[first : first + narrow, :].astype(bf16)


def backward(bas, grad_state, low, high, wide, capacity, lists):
    edges, narrow = grad_state.shape
    rho = low.shape[1]
    padded = bas.shape[1]
    block = 256
    sub = 64
    home = edges // capacity * narrow
    rows = home + lists * narrow
    resident = lambda *shape: pl.BlockSpec(shape, lambda i: (0,) * len(shape))
    return pl.pallas_call(
        functools.partial(backward_kernel, sub, lists),
        grid=(edges // block,),
        out_shape=(jax.ShapeDtypeStruct((home, capacity), f32),)
        + (jax.ShapeDtypeStruct((narrow, capacity), bf16),) * lists,
        in_specs=[
            pl.BlockSpec((block * rho // GROUP, padded), lambda i: (i, 0)),
            pl.BlockSpec((block, narrow), lambda i: (i, 0)),
            pl.BlockSpec((block // GROUP, rho), lambda i: (i, 0)),
            pl.BlockSpec((block // GROUP, rho), lambda i: (i, 0)),
            resident(*wide.shape),
        ],
        out_specs=(resident(home, capacity),) + (resident(narrow, capacity),) * lists,
        scratch_shapes=[
            pltpu.VMEM((rows, capacity), f32),
            pltpu.VMEM((block * narrow, padded), bf16),
            pltpu.VMEM((rows, sub // GROUP * rho), bf16),
            pltpu.VMEM((capacity, sub // GROUP * rho), bf16),
            pltpu.VMEM((capacity, rho), bf16),
        ],
        compiler_params=params(32),
        cost_estimate=cost(edges, 32),
        name="backward",
    )(bas, grad_state, low, high, wide)


def tail_kernel(
    scale, parts, lists,
    count_ref, core_ref, pool_ref, rows_ref, pdt_ref, pre_ref, hid_ref, x_ref, we_ref, wd_ref, *rest
):
    back_refs = rest[:lists]
    out_ref, keep_ref, give_ref, grad_s = rest[lists:]
    narrow, edges = pdt_ref.shape
    capacity = back_refs[0].shape[1]
    model = pre_ref.shape[1]
    grad = jnp.concatenate(
        [pool_ref[h * narrow : (h + 1) * narrow, :] for h in range(edges // capacity)], axis=1
    )
    for which, back_ref in enumerate(back_refs):
        grad = grad + mm(back_ref[...], send_hot(rows_ref, count_ref, which, edges), NT)
    grad_down = (grad * silu_slope(pdt_ref[...])).astype(bf16)
    step = 256
    for start in range(0, edges, step):
        part = slice(start, start + step)
        grad_hidden = mm(grad_down[:, part], wd_ref[...], TN)
        grad_edge = (grad_hidden * silu_slope(pre_ref[part, :])).astype(bf16)
        grad_s[part, :] = grad_edge
        out_ref[0, part, :] = mm(grad_edge, we_ref[...], NT).astype(bf16)
    down = lax.dot_general(
        hid_ref[...], grad_down, (((0,), (1,)), ((), ())), preferred_element_type=f32
    )
    down = jnp.concatenate([down, jnp.zeros_like(down)], axis=1)
    span = model // parts
    for start in range(0, model, step):
        edge = mm(x_ref[0, :, start : start + step], grad_s[...], TN)
        both = jnp.concatenate([edge, down[start : start + step, :]], axis=1) * scale
        for first in range(0, step, 2 * span):
            settle(
                core_ref, keep_ref, give_ref, (start + first) // (2 * span), slice(None),
                both[first : first + span, :], both[first + span : first + 2 * span, :],
            )


def tail(pool, back, rows, counts, core, pdt, pre, hidden, messages, w_edge, w_down, scale, parts):
    _, edges, model = messages.shape
    narrow = w_down.shape[0]
    share = jax.ShapeDtypeStruct((parts // 2, model // parts, model + 2 * narrow), bf16)
    return pl.pallas_call(
        functools.partial(tail_kernel, scale, parts, len(back)),
        out_shape=(
            jax.ShapeDtypeStruct((1, edges, model), bf16),
            share,
            share,
        ),
        in_specs=[smem(), smem()] + [vmem()] * (8 + len(back)),
        out_specs=(vmem(),) * 3,
        scratch_shapes=[pltpu.VMEM((edges, model), bf16)],
        compiler_params=params(),
        cost_estimate=cost(edges, 4),
        name="tail",
    )(counts, core, pool, rows, pdt, pre, hidden, messages, w_edge, w_down, *back)


def add_pair_kernel(chip_ref, keep_ref, got_ref, mine_ref, *out_refs):
    chips = keep_ref.shape[0]
    chip = chip_ref[0, 0]
    for step, out_ref in enumerate((mine_ref,) + out_refs):
        at = lax.rem(chip + step, chips)
        out_ref[...] = (keep_ref[at].astype(f32) + got_ref[at].astype(f32)).astype(bf16)


def add_kernel(*refs):
    *in_refs, out_ref = refs
    total = in_refs[0][...].astype(f32)
    for in_ref in in_refs[1:]:
        total = total + in_ref[...].astype(f32)
    out_ref[...] = total.astype(bf16)


def over_graph(keep, give, chip):
    chips, height, wide = keep.shape
    devices = 2 * chips
    piece = jax.ShapeDtypeStruct((height, wide), bf16)
    got = lax.ppermute(give, "graph", [(i, i ^ 1) for i in range(devices)])
    mine, *sends = pl.pallas_call(
        add_pair_kernel,
        out_shape=(piece,) * chips,
        in_specs=[smem(), vmem(), vmem()],
        out_specs=(vmem(),) * chips,
        compiler_params=params(),
    )(chip, keep, got)
    arrived = []
    for step, send in enumerate(sends):
        route = [(i, (i + 2 * (step + 1)) % devices) for i in range(devices)]
        arrived.append(lax.ppermute(send, "graph", route))
    return pl.pallas_call(
        add_kernel,
        out_shape=piece,
        in_specs=[vmem()] * chips,
        out_specs=vmem(),
        compiler_params=params(),
    )(mine, *arrived)


def over_dp(share):
    slabs = lax.axis_size("dp")
    copies = [share]
    for step in range(1, slabs):
        copies.append(lax.ppermute(share, "dp", [(i, i ^ step) for i in range(slabs)]))
    return copies


def paired_sum(values):
    while len(values) > 1:
        values = [values[i] + values[i + 1] for i in range(0, len(values), 2)]
    return values[0]


def finish_kernel(slabs, *refs):
    early_refs, late_refs = refs[:slabs], refs[slabs : 2 * slabs]
    edge_ref, down_ref, bil_ref, up_ref = refs[2 * slabs :]
    rows, model = edge_ref.shape
    basis = bil_ref.shape[0]
    _, narrow, _ = up_ref.shape
    padded = 128
    span = bil_ref.shape[1] // narrow * padded

    def total(in_refs, *part):
        return paired_sum([in_ref[part].astype(f32) for in_ref in in_refs])

    every = slice(None)
    for c in range(bil_ref.shape[1] // narrow):
        block = total(early_refs, every, slice(c * padded, (c + 1) * padded))
        bil_ref[:, c * narrow : (c + 1) * narrow] = block.T[:basis, :]
    both = total(early_refs, slice(0, rows), slice(span, span + 2 * narrow)).T
    up_ref[0] = both[:narrow, :]
    up_ref[1] = both[narrow:, :]
    edge_ref[...] = total(late_refs, every, slice(0, model))
    down_ref[...] = total(late_refs, every, slice(model, model + 2 * narrow))[:, :narrow]


def finish(early, late, basis, narrow, model, parts):
    rows = model // parts
    return pl.pallas_call(
        functools.partial(finish_kernel, len(early)),
        out_shape=(
            jax.ShapeDtypeStruct((rows, model), f32),
            jax.ShapeDtypeStruct((rows, narrow), f32),
            jax.ShapeDtypeStruct((basis, narrow * narrow // parts), f32),
            jax.ShapeDtypeStruct((2, narrow, rows), f32),
        ),
        in_specs=[vmem()] * (len(early) + len(late)),
        out_specs=(vmem(),) * 4,
        compiler_params=params(),
        name="finish",
    )(*early, *late)


def body(
    messages,
    cotangent,
    triplet_basis,
    w_edge,
    w_down,
    w_bil,
    w_up,
    trip_src,
    send_rows,
    send_count,
    rev_src,
    edge_count,
):
    _, edges, model = messages.shape
    narrow = w_down.shape[1]
    w_down = w_down.T
    slots = trip_src.shape[2]
    _, lists, capacity = send_rows.shape
    basis_count = w_bil.shape[0]
    parts = lax.axis_size("graph")
    scale = 1.0 / math.sqrt(lax.axis_size("dp") * parts * edges)
    shifts = offsets(lists)
    place = lax.axis_index("graph").reshape(1, 1)
    core, chip = place % 2, place // 2

    def exchange(blocks, sign):
        moved = []
        for which in range(lists):
            moved.append(shifted(blocks[which], "graph", sign * shifts[which]))
        return moved

    pre, hidden, pdt, red, *send_red = front(messages, w_edge, w_down, send_rows, send_count)
    recv_red = exchange(send_red, 1)
    low, high, *send_cot = pick(cotangent, send_rows, send_count, trip_src, red)
    recv_cot = exchange(send_cot, 1)
    bas = align(triplet_basis, basis_count, slots, send_cot[0])
    outer, state, wide = forward(bas, low, high, red, recv_red, w_bil)
    grad_state, up = state_grads(edge_count, state, cotangent, rev_src, recv_cot, w_up)
    keep, give = bil_shares(core, outer, grad_state, up, scale, parts)
    early = over_graph(keep, give, chip)
    home, *returned = backward(bas, grad_state, low, high, wide, capacity, lists)
    back = exchange(returned, -1)
    early = over_dp(early)
    grad_messages, keep, give = tail(
        home, back, send_rows, send_count, core, pdt, pre, hidden, messages, w_edge, w_down,
        scale, parts,
    )
    late = over_dp(over_graph(keep, give, chip))
    edge_out, down_out, bil_out, up_out = finish(early, late, basis_count, narrow, model, parts)
    return (grad_messages, edge_out, down_out, bil_out, up_out)


def solution(mesh):
    return jax.shard_map(
        body,
        mesh=mesh,
        in_specs=(
            P("dp", "graph", None),
            P("dp", "graph", None),
            P("dp", "graph", None),
            P(),
            P(),
            P(),
            P(),
            P("dp", "graph", None),
            P("dp", "graph", None),
            P("dp", "graph"),
            P("dp", "graph"),
            P("dp", "graph"),
        ),
        out_specs=(
            P("dp", "graph", None),
            P("graph", None),
            P("graph", None),
            P(None, "graph"),
            P(None, None, "graph"),
        ),
        check_vma=False,
    )
```

```python
import functools
import math

import jax
import jax.numpy as jnp
from jax import lax
from jax.experimental import pallas as pl
from jax.experimental.pallas import tpu as pltpu
from jax.sharding import PartitionSpec as P


inv_root = 0.7071067811865476
bf16 = jnp.bfloat16
f32 = jnp.float32
GROUP = 8
NN = (((1,), (0,)), ((), ()))
NT = (((1,), (1,)), ((), ()))
TN = (((0,), (0,)), ((), ()))


def mm(left, right, dims=NN):
    return lax.dot_general(left, right, dims, preferred_element_type=f32)


def silu_slope(values):
    sigma = jax.nn.sigmoid(values)
    return sigma * (1.0 + values * (1.0 - sigma))


def offsets(count):
    return [(which // 2 + 1) * (1 - 2 * (which % 2)) for which in range(count)]


def shifted(block, axis, distance):
    devices = range(lax.axis_size(axis))
    route = [((i - distance) % len(devices), i) for i in devices]
    return lax.ppermute(block, axis, route)


def iota(shape, dim):
    return lax.broadcasted_iota(jnp.int32, shape, dim)


def one_hot(index, shape, dim):
    return jnp.where(index == iota(shape, dim), 1.0, 0.0).astype(bf16)


def vmem():
    return pl.BlockSpec(memory_space=pltpu.VMEM)


def params(mib=12):
    return pltpu.CompilerParams(vmem_limit_bytes=mib * 1024 * 1024)


def cost(edges, weight):
    return pl.CostEstimate(
        flops=weight * edges * 10**6, transcendentals=0, bytes_accessed=weight * edges * 1000
    )


def send_hot(rows_ref, count_ref, which, edges):
    capacity = rows_ref.shape[2]
    rows = rows_ref[0, which : which + 1, :]
    used = iota((1, capacity), 1) < count_ref[0, which]
    return one_hot(jnp.where(used, rows, -1), (edges, capacity), 0)


def front_kernel(
    count_ref, x_ref, we_ref, wd_ref, rows_ref, pre_ref, hid_ref, pdt_ref, red_ref, *send_refs
):
    edges = x_ref.shape[1]
    step = 256
    for start in range(0, edges, step):
        pre = mm(x_ref[0, start : start + step, :], we_ref[...])
        pre_ref[start : start + step, :] = pre
        hidden = (pre * jax.nn.sigmoid(pre)).astype(bf16)
        hid_ref[start : start + step, :] = hidden
        down = mm(wd_ref[...], hidden, NT)
        pdt_ref[:, start : start + step] = down
        red_ref[:, start : start + step] = (down * jax.nn.sigmoid(down)).astype(bf16)
    for which, send_ref in enumerate(send_refs):
        hot = send_hot(rows_ref, count_ref, which, edges)
        send_ref[...] = mm(red_ref[...], hot).astype(bf16)


def smem():
    return pl.BlockSpec(memory_space=pltpu.SMEM)


def front(messages, w_edge, w_down, rows, counts):
    _, edges, model = messages.shape
    narrow = w_down.shape[0]
    _, lists, capacity = rows.shape
    return pl.pallas_call(
        front_kernel,
        out_shape=(
            jax.ShapeDtypeStruct((edges, model), f32),
            jax.ShapeDtypeStruct((edges, model), bf16),
            jax.ShapeDtypeStruct((narrow, edges), f32),
            jax.ShapeDtypeStruct((narrow, edges), bf16),
        )
        + (jax.ShapeDtypeStruct((narrow, capacity), bf16),) * lists,
        in_specs=[smem()] + [vmem()] * 4,
        out_specs=(vmem(),) * (4 + lists),
        compiler_params=params(56),
        cost_estimate=cost(edges, 3),
        name="front",
    )(counts, messages, w_edge, w_down, rows)


def pick_kernel(count_ref, cot_ref, rows_ref, trip_ref, after_ref, low_ref, high_ref, *send_refs):
    edges = cot_ref.shape[1]
    capacity = rows_ref.shape[2]
    groups, rho = low_ref.shape
    slots = rho // GROUP
    trip = trip_ref[0]
    repeat = one_hot(iota((slots, rho), 1) // GROUP, (slots, rho), 0)
    own = iota((edges, rho), 0) % GROUP == iota((edges, rho), 1) % GROUP
    gather = one_hot(iota((groups, edges), 1) // GROUP, (groups, edges), 0)

    def slot_major(values):
        spread = mm(values.astype(f32).astype(bf16), repeat)
        return mm(gather, jnp.where(own, spread, 0.0).astype(bf16))

    low_ref[...] = slot_major(jnp.bitwise_and(trip, capacity - 1))
    high_ref[...] = slot_major(jnp.right_shift(trip, capacity.bit_length() - 1)).astype(jnp.int32)
    for which, send_ref in enumerate(send_refs):
        hot = send_hot(rows_ref, count_ref, which, edges)
        send_ref[...] = mm(hot, cot_ref[0], TN).astype(bf16)


def pick(cotangent, rows, counts, trips, after):
    _, edges, model = cotangent.shape
    _, lists, capacity = rows.shape
    slot_major = (edges // GROUP, trips.shape[2] * GROUP)
    return pl.pallas_call(
        pick_kernel,
        out_shape=(
            jax.ShapeDtypeStruct(slot_major, f32),
            jax.ShapeDtypeStruct(slot_major, jnp.int32),
        )
        + (jax.ShapeDtypeStruct((capacity, model), bf16),) * lists,
        in_specs=[smem(), vmem(), vmem(), vmem(), pl.BlockSpec(memory_space=pl.ANY)],
        out_specs=(vmem(),) * (2 + lists),
        compiler_params=params(12),
        cost_estimate=cost(edges, 3),
        name="pick",
    )(counts, cotangent, rows, trips, after)


def widen_weights(wb_ref, wide):
    basis, _ = wb_ref.shape
    narrow = wide.shape[1]
    padded = wide.shape[0] // narrow
    zeros = jnp.zeros((padded - basis, narrow), bf16)
    for c in range(0, narrow, 2):
        pair = wb_ref[:, c * narrow : (c + 2) * narrow]
        wide[c * padded : (c + 1) * padded, :] = jnp.concatenate(
            [pair[:, :narrow], zeros], axis=0
        )
        wide[(c + 1) * padded : (c + 2) * padded, :] = jnp.concatenate(
            [pair[:, narrow:], zeros], axis=0
        )


def low_iota(capacity, rho):
    return iota((capacity, rho), 0).astype(f32).astype(bf16)


def low_hot(low, numbers):
    one, zero = jnp.ones((), bf16), jnp.zeros((), bf16)
    return jnp.where(low == numbers, one, zero)


def align_kernel(basis_count, sub, after_ref, basis_ref, bas_ref, slot_s):
    groups, rho, _ = slot_s.shape
    slots = rho // GROUP

    def body(index, carry):
        x = basis_ref[0, pl.ds(pl.multiple_of(index * sub, sub), sub), :].astype(f32)
        for k in range(slots):
            tile, off = divmod(k * basis_count, 128)
            if off + basis_count <= 128:
                part = x[:, tile * 128 : tile * 128 + 128]
                if off:
                    part = pltpu.roll(part, 128 - off, 1)
            else:
                part = pltpu.roll(x[:, tile * 128 : tile * 128 + 256], 256 - off, 1)[:, :128]
            for g in range(groups):
                slot_s[g, k * GROUP : (k + 1) * GROUP, :] = part[g * GROUP : (g + 1) * GROUP, :]
        for g in range(groups):
            first = pl.multiple_of((index * groups + g) * rho, rho)
            bas_ref[pl.ds(first, rho), :] = slot_s[g].astype(bf16)
        return carry

    lax.fori_loop(0, basis_ref.shape[1] // sub, body, 0)


def align(triplet_basis, basis_count, slots, after):
    _, edges, wide = triplet_basis.shape
    rho = slots * GROUP
    padded = 128
    block = 128
    sub = 64
    return pl.pallas_call(
        functools.partial(align_kernel, basis_count, sub),
        grid=(edges // block,),
        out_shape=jax.ShapeDtypeStruct((edges * slots, padded), bf16),
        in_specs=[
            pl.BlockSpec(memory_space=pl.ANY),
            pl.BlockSpec((1, block, wide), lambda i: (0, i, 0)),
        ],
        out_specs=pl.BlockSpec((block * slots, padded), lambda i: (i, 0)),
        scratch_shapes=[pltpu.VMEM((sub // GROUP, rho, padded), f32)],
        compiler_params=params(12),
        cost_estimate=cost(edges, 6),
        name="align",
    )(after, triplet_basis)


def halves(bas):
    first = iota(bas.shape, 0) % GROUP < GROUP // 2
    zero = jnp.zeros_like(bas)
    return jnp.concatenate([jnp.where(first, bas, zero), jnp.where(first, zero, bas)], axis=1)


def forward_kernel(sub, lists, bas_ref, low_ref, high_ref, red_ref, wb_ref, *rest):
    recv_refs = rest[:lists]
    outer_ref, state_ref, wide, pool, gat_s, num_s = rest[lists:]
    narrow, edges = red_ref.shape
    capacity = recv_refs[0].shape[1]
    rho = low_ref.shape[1]
    padded = bas_ref.shape[1]
    locals_ = edges // capacity

    @pl.when(pl.program_id(0) == 0)
    def _():
        for h in range(locals_):
            pool[h * narrow : (h + 1) * narrow, :] = red_ref[:, h * capacity : (h + 1) * capacity]
        for h in range(lists):
            pool[(locals_ + h) * narrow : (locals_ + h + 1) * narrow, :] = recv_refs[h][...]
        widen_weights(wb_ref, wide)
        num_s[...] = low_iota(capacity, rho)

    groups = sub // GROUP
    own = iota((GROUP, rho), 1) % GROUP == iota((GROUP, rho), 0)

    def body(index, carry):
        first = pl.multiple_of(index * sub, sub)
        first_group = pl.multiple_of(index * groups, groups)

        def gather(g):
            low = low_ref[pl.ds(first_group + g, 1), :].astype(bf16)
            high = high_ref[pl.ds(first_group + g, 1), :]
            found = mm(pool[...], low_hot(low, num_s[...]))
            gathered = jnp.zeros((narrow, rho), f32)
            for h in range(locals_ + lists):
                gathered = jnp.where(high == h, found[h * narrow : (h + 1) * narrow, :], gathered)
            gat_s[g] = gathered

        def product(g):
            spread = jnp.concatenate(
                [
                    jnp.where(own, gat_s[g, pl.ds(c, GROUP, stride=0), :], 0.0)
                    for c in range(narrow)
                ],
                axis=0,
            ).astype(bf16)
            bas = bas_ref[pl.ds(pl.multiple_of((first_group + g) * rho, rho), rho), :]
            return mm(spread, bas)

        gather(0)
        held = None
        for g in range(groups):
            if g + 1 < groups:
                gather(g + 1)
            outer = product(g)
            if g % 2 == 0:
                held = outer
                continue
            rows = pl.ds(pl.multiple_of(first + (g - 1) * GROUP, 2 * GROUP), 2 * GROUP)
            for c in range(narrow):
                part = slice(c * GROUP, (c + 1) * GROUP)
                outer_ref[rows, c * padded : (c + 1) * padded] = jnp.concatenate(
                    [held[part, :], outer[part, :]], axis=0
                ).astype(bf16)
        return carry

    lax.fori_loop(0, outer_ref.shape[0] // sub, body, 0)
    state_ref[...] = mm(outer_ref[...], wide[...]).astype(bf16)


def forward(bas, low, high, red, recv, w_bil):
    narrow, edges = red.shape
    lists = len(recv)
    capacity = recv[0].shape[1]
    rho = low.shape[1]
    padded = bas.shape[1]
    block = 256
    sub = 64
    resident = lambda *shape: pl.BlockSpec(shape, lambda i: (0,) * len(shape))
    return pl.pallas_call(
        functools.partial(forward_kernel, sub, lists),
        grid=(edges // block,),
        out_shape=(
            jax.ShapeDtypeStruct((edges, narrow * padded), bf16),
            jax.ShapeDtypeStruct((edges, narrow), bf16),
            jax.ShapeDtypeStruct((narrow * padded, narrow), bf16),
        ),
        in_specs=[
            pl.BlockSpec((block * rho // GROUP, padded), lambda i: (i, 0)),
            pl.BlockSpec((block // GROUP, rho), lambda i: (i, 0)),
            pl.BlockSpec((block // GROUP, rho), lambda i: (i, 0)),
            resident(narrow, edges),
            resident(*w_bil.shape),
        ]
        + [resident(narrow, capacity)] * lists,
        out_specs=(
            pl.BlockSpec((block, narrow * padded), lambda i: (i, 0)),
            pl.BlockSpec((block, narrow), lambda i: (i, 0)),
            resident(narrow * padded, narrow),
        ),
        scratch_shapes=[
            pltpu.VMEM((edges // capacity * narrow + lists * narrow, capacity), bf16),
            pltpu.VMEM((sub // GROUP, narrow, rho), f32),
            pltpu.VMEM((capacity, rho), bf16),
        ],
        compiler_params=params(32),
        cost_estimate=cost(edges, 29),
        name="forward",
    )(bas, low, high, red, w_bil, *recv)


def settle(core_ref, keep_ref, give_ref, pair, part, even, odd):
    is_odd = core_ref[0, 0] == 1
    keep_ref[pair, :, part] = jnp.where(is_odd, odd, even).astype(bf16)
    give_ref[pair, :, part] = jnp.where(is_odd, even, odd).astype(bf16)


def state_kernel(
    lists, count_ref, state_ref, cot_ref, rev_ref, own_ref, wu_ref, *rest
):
    recv_refs = rest[:lists]
    grad_ref, up_ref, mirror_s, cast_s = rest[lists:]
    block, _ = state_ref.shape
    edges = own_ref.shape[1]
    capacity, model = recv_refs[0].shape
    pid = pl.program_id(0)

    @pl.when(pid == 0)
    def _():
        up_ref[...] = jnp.zeros_like(up_ref)

    row = rev_ref[...].astype(f32)
    reverse = jnp.broadcast_to(row, (GROUP, block)).T[:, :1].astype(jnp.int32)
    mirror = mm(one_hot(reverse, (block, edges), 1), own_ref[0])
    for which, recv_ref in enumerate(recv_refs):
        base = edges + which * capacity
        mirror = mirror + mm(one_hot(reverse - base, (block, capacity), 1), recv_ref[...])
    mirror_s[...] = mirror
    step = 64
    for start in range(0, block, step):
        part = slice(start, start + step)
        state = state_ref[part, :]
        alive = pid * block + start + iota((step, 1), 0) < count_ref[0, 0]
        scaled = jnp.where(alive, cot_ref[0, part, :].astype(f32) * inv_root, 0.0)
        cast_s[part, :model] = (scaled * silu_slope(mm(state, wu_ref[0]))).astype(bf16)
        cast_s[part, model:] = (
            mirror_s[part, :] * inv_root * silu_slope(mm(state, wu_ref[1]))
        ).astype(bf16)
    up_ref[...] += mm(state_ref[...], cast_s[...], TN)
    back_rev = mm(cast_s[:, model:], wu_ref[1], NT).astype(bf16).astype(f32)
    grad_ref[...] = (mm(cast_s[:, :model], wu_ref[0], NT) + back_rev).astype(bf16)


def state_grads(count, state, cotangent, rev, recv_cot, w_up):
    edges, narrow = state.shape
    model = cotangent.shape[2]
    block = 256
    lists = len(recv_cot)
    resident = lambda *shape: pl.BlockSpec(shape, lambda i: (0,) * len(shape))
    return pl.pallas_call(
        functools.partial(state_kernel, lists),
        grid=(edges // block,),
        out_shape=(
            jax.ShapeDtypeStruct((edges, narrow), bf16),
            jax.ShapeDtypeStruct((narrow, 2 * model), f32),
        ),
        in_specs=[
            smem(),
            pl.BlockSpec((block, narrow), lambda i: (i, 0)),
            pl.BlockSpec((1, block, model), lambda i: (0, i, 0)),
            pl.BlockSpec((1, block), lambda i: (0, i)),
            resident(1, edges, model),
            resident(*w_up.shape),
        ]
        + [resident(*recv_cot[0].shape)] * lists,
        out_specs=(
            pl.BlockSpec((block, narrow), lambda i: (i, 0)),
            resident(narrow, 2 * model),
        ),
        scratch_shapes=[
            pltpu.VMEM((block, model), f32),
            pltpu.VMEM((block, 2 * model), bf16),
        ],
        compiler_params=params(16),
        cost_estimate=cost(edges, 7),
        name="state_grads",
    )(count, state, cotangent, rev, cotangent, w_up, *recv_cot)


def bil_kernel(scale, parts, core_ref, outer_ref, grad_ref, up_ref, keep_ref, give_ref, bil_s):
    narrow, columns = bil_s.shape
    model = up_ref.shape[1] // 2
    pid = pl.program_id(0)

    @pl.when(pid == 0)
    def _():
        bil_s[...] = jnp.zeros_like(bil_s)

    wide_step = 1024
    for start in range(0, columns, wide_step):
        bil_s[:, start : start + wide_step] += mm(
            grad_ref[...], outer_ref[:, start : start + wide_step], TN
        )

    @pl.when(pid == pl.num_programs(0) - 1)
    def _():
        span = columns // parts
        thin = model // parts
        both = jnp.concatenate([up_ref[:, :model], up_ref[:, model:]], axis=0).T
        if thin < narrow:
            spare = jnp.zeros((narrow - thin, 2 * narrow), f32)
        for pair in range(parts // 2):
            even = slice(2 * pair * span, (2 * pair + 1) * span)
            odd = slice((2 * pair + 1) * span, (2 * pair + 2) * span)
            settle(core_ref, keep_ref, give_ref, pair, slice(0, span),
                   bil_s[:, even] * scale, bil_s[:, odd] * scale)
            sides = []
            for dest in (2 * pair, 2 * pair + 1):
                piece = both[dest * thin : (dest + 1) * thin, :] * scale
                if thin < narrow:
                    piece = jnp.concatenate([piece, spare], axis=0)
                sides.append(piece)
            settle(core_ref, keep_ref, give_ref, pair, slice(span, span + 2 * narrow), *sides)


def bil_shares(core, outer, grad_state, up, scale, parts):
    edges, narrow = grad_state.shape
    columns = outer.shape[1]
    block = 256
    share = (parts // 2, narrow, columns // parts + 2 * narrow)
    resident = lambda *shape: pl.BlockSpec(shape, lambda i: (0,) * len(shape))
    return pl.pallas_call(
        functools.partial(bil_kernel, scale, parts),
        grid=(edges // block,),
        out_shape=(jax.ShapeDtypeStruct(share, bf16),) * 2,
        in_specs=[
            smem(),
            pl.BlockSpec((block, columns), lambda i: (i, 0)),
            pl.BlockSpec((block, narrow), lambda i: (i, 0)),
            resident(*up.shape),
        ],
        out_specs=(resident(*share),) * 2,
        scratch_shapes=[pltpu.VMEM((narrow, columns), f32)],
        compiler_params=params(20),
        cost_estimate=cost(edges, 4),
        name="bil_shares",
    )(core, outer, grad_state, up)


def own_rows(mixed, narrow):
    rho = mixed.shape[1]
    half = GROUP // 2
    value = mixed.reshape(narrow // GROUP, half, GROUP, rho)
    shape = (1, 1, GROUP, rho)
    row, lane = iota(shape, 2), iota(shape, 3)
    step = half // 2
    while step:
        low, high = value[:, :step], value[:, step:]
        upper = jnp.bitwise_and(row, step) > 0
        kept = jnp.bitwise_and(row, step) == jnp.bitwise_and(lane, step)
        straight = jnp.where(upper, high, low)
        other = jnp.where(upper, low, high)
        moved = jnp.where(
            upper, pltpu.roll(other, step, 2), pltpu.roll(other, GROUP - step, 2)
        )
        value = jnp.where(kept, straight, moved)
        step //= 2
    return value.reshape(narrow, rho)


def backward_kernel(sub, lists, bas_ref, grad_ref, low_ref, high_ref, wide, home_ref, *rest):
    back_refs = rest[:lists]
    pool_s, turn_s, cast_s, hot_s, num_s = rest[lists:]
    block, narrow = grad_ref.shape
    padded = bas_ref.shape[1]
    rho = low_ref.shape[1]
    rows, capacity = pool_s.shape
    pid = pl.program_id(0)

    @pl.when(pid == 0)
    def _():
        pool_s[...] = jnp.zeros_like(pool_s)
        num_s[...] = low_iota(capacity, rho)

    grad_state = grad_ref[...]
    half = GROUP // 2
    height = narrow * half
    top = iota((GROUP, 1), 0) < half

    def spread(tile, carry):
        start = pl.multiple_of(tile * GROUP * padded, GROUP * padded)
        grad = mm(grad_state, wide[pl.ds(start, GROUP * padded), :], NT)
        for g in range(block // GROUP):
            part = slice(g * GROUP, (g + 1) * GROUP)
            sides = []
            for c in range(half):
                near = grad[part, c * padded : (c + 1) * padded]
                far = grad[part, (c + half) * padded : (c + half + 1) * padded]
                left = jnp.where(top, near, pltpu.roll(far, half, 0))
                right = jnp.where(top, pltpu.roll(near, half, 0), far)
                sides.append(jnp.concatenate([left, right], axis=1))
            at = pl.multiple_of(g * height + tile * GROUP * half, GROUP * half)
            turn_s[pl.ds(at, GROUP * half), :] = jnp.concatenate(sides, axis=0).astype(bf16)
        return carry

    lax.fori_loop(0, narrow // GROUP, spread, 0, unroll=2)
    groups = sub // GROUP

    def body(index, carry):
        first_group = pl.multiple_of(index * groups, groups)

        def mix(g):
            here = first_group + g
            bas = bas_ref[pl.ds(pl.multiple_of(here * rho, rho), rho), :]
            grads = turn_s[pl.ds(pl.multiple_of(here * height, height), height), :]
            return mm(grads, halves(bas), NT)

        def cast(g, mixed):
            trip_grad = own_rows(mixed, narrow).astype(bf16)
            low = low_ref[pl.ds(first_group + g, 1), :].astype(bf16)
            high = high_ref[pl.ds(first_group + g, 1), :]
            part = slice(g * rho, (g + 1) * rho)
            hot_s[:, part] = low_hot(low, num_s[...])
            zero = jnp.zeros_like(trip_grad)
            wide_high = jnp.broadcast_to(high.astype(f32).astype(bf16), trip_grad.shape)
            for h in range(rows // narrow):
                cast_s[h * narrow : (h + 1) * narrow, part] = jnp.where(
                    wide_high == jnp.asarray(h, bf16), trip_grad, zero
                )

        ready = mix(0)
        for g in range(groups):
            mixed = ready
            if g + 1 < groups:
                ready = mix(g + 1)
            cast(g, mixed)
        pool_s[...] += mm(cast_s[...], hot_s[...], NT)
        return carry

    lax.fori_loop(0, block // sub, body, 0)

    @pl.when(pid == pl.num_programs(0) - 1)
    def _():
        home = home_ref.shape[0]
        home_ref[...] = pool_s[:home, :]
        for which, back_ref in enumerate(back_refs):
            first = home + which * narrow
            back_ref[...] = pool_s[first : first + narrow, :].astype(bf16)


def backward(bas, grad_state, low, high, wide, capacity, lists):
    edges, narrow = grad_state.shape
    rho = low.shape[1]
    padded = bas.shape[1]
    block = 256
    sub = 64
    home = edges // capacity * narrow
    rows = home + lists * narrow
    resident = lambda *shape: pl.BlockSpec(shape, lambda i: (0,) * len(shape))
    return pl.pallas_call(
        functools.partial(backward_kernel, sub, lists),
        grid=(edges // block,),
        out_shape=(jax.ShapeDtypeStruct((home, capacity), f32),)
        + (jax.ShapeDtypeStruct((narrow, capacity), bf16),) * lists,
        in_specs=[
            pl.BlockSpec((block * rho // GROUP, padded), lambda i: (i, 0)),
            pl.BlockSpec((block, narrow), lambda i: (i, 0)),
            pl.BlockSpec((block // GROUP, rho), lambda i: (i, 0)),
            pl.BlockSpec((block // GROUP, rho), lambda i: (i, 0)),
            resident(*wide.shape),
        ],
        out_specs=(resident(home, capacity),) + (resident(narrow, capacity),) * lists,
        scratch_shapes=[
            pltpu.VMEM((rows, capacity), f32),
            pltpu.VMEM((block * narrow // 2, 2 * padded), bf16),
            pltpu.VMEM((rows, sub // GROUP * rho), bf16),
            pltpu.VMEM((capacity, sub // GROUP * rho), bf16),
            pltpu.VMEM((capacity, rho), bf16),
        ],
        compiler_params=params(32),
        cost_estimate=cost(edges, 32),
        name="backward",
    )(bas, grad_state, low, high, wide)


def tail_kernel(
    scale, parts, lists,
    count_ref, core_ref, pool_ref, rows_ref, pdt_ref, pre_ref, hid_ref, x_ref, we_ref, wd_ref, *rest
):
    back_refs = rest[:lists]
    out_ref, keep_ref, give_ref, grad_s = rest[lists:]
    narrow, edges = pdt_ref.shape
    capacity = back_refs[0].shape[1]
    model = pre_ref.shape[1]
    grad = jnp.concatenate(
        [pool_ref[h * narrow : (h + 1) * narrow, :] for h in range(edges // capacity)], axis=1
    )
    for which, back_ref in enumerate(back_refs):
        grad = grad + mm(back_ref[...], send_hot(rows_ref, count_ref, which, edges), NT)
    grad_down = (grad * silu_slope(pdt_ref[...])).astype(bf16)
    step = 256
    for start in range(0, edges, step):
        part = slice(start, start + step)
        grad_hidden = mm(grad_down[:, part], wd_ref[...], TN)
        grad_edge = (grad_hidden * silu_slope(pre_ref[part, :])).astype(bf16)
        grad_s[part, :] = grad_edge
        out_ref[0, part, :] = mm(grad_edge, we_ref[...], NT).astype(bf16)
    down = lax.dot_general(
        hid_ref[...], grad_down, (((0,), (1,)), ((), ())), preferred_element_type=f32
    )
    down = jnp.concatenate([down, jnp.zeros_like(down)], axis=1)
    span = model // parts
    for start in range(0, model, step):
        edge = mm(x_ref[0, :, start : start + step], grad_s[...], TN)
        both = jnp.concatenate([edge, down[start : start + step, :]], axis=1) * scale
        for first in range(0, step, 2 * span):
            settle(
                core_ref, keep_ref, give_ref, (start + first) // (2 * span), slice(None),
                both[first : first + span, :], both[first + span : first + 2 * span, :],
            )


def tail(pool, back, rows, counts, core, pdt, pre, hidden, messages, w_edge, w_down, scale, parts):
    _, edges, model = messages.shape
    narrow = w_down.shape[0]
    share = jax.ShapeDtypeStruct((parts // 2, model // parts, model + 2 * narrow), bf16)
    return pl.pallas_call(
        functools.partial(tail_kernel, scale, parts, len(back)),
        out_shape=(
            jax.ShapeDtypeStruct((1, edges, model), bf16),
            share,
            share,
        ),
        in_specs=[smem(), smem()] + [vmem()] * (8 + len(back)),
        out_specs=(vmem(),) * 3,
        scratch_shapes=[pltpu.VMEM((edges, model), bf16)],
        compiler_params=params(),
        cost_estimate=cost(edges, 4),
        name="tail",
    )(counts, core, pool, rows, pdt, pre, hidden, messages, w_edge, w_down, *back)


def add_pair_kernel(chip_ref, keep_ref, got_ref, mine_ref, *out_refs):
    chips = keep_ref.shape[0]
    chip = chip_ref[0, 0]
    for step, out_ref in enumerate((mine_ref,) + out_refs):
        at = lax.rem(chip + step, chips)
        out_ref[...] = (keep_ref[at].astype(f32) + got_ref[at].astype(f32)).astype(bf16)


def add_kernel(*refs):
    *in_refs, out_ref = refs
    total = in_refs[0][...].astype(f32)
    for in_ref in in_refs[1:]:
        total = total + in_ref[...].astype(f32)
    out_ref[...] = total.astype(bf16)


def over_graph(keep, give, chip):
    chips, height, wide = keep.shape
    devices = 2 * chips
    piece = jax.ShapeDtypeStruct((height, wide), bf16)
    got = lax.ppermute(give, "graph", [(i, i ^ 1) for i in range(devices)])
    mine, *sends = pl.pallas_call(
        add_pair_kernel,
        out_shape=(piece,) * chips,
        in_specs=[smem(), vmem(), vmem()],
        out_specs=(vmem(),) * chips,
        compiler_params=params(),
    )(chip, keep, got)
    arrived = []
    for step, send in enumerate(sends):
        route = [(i, (i + 2 * (step + 1)) % devices) for i in range(devices)]
        arrived.append(lax.ppermute(send, "graph", route))
    return pl.pallas_call(
        add_kernel,
        out_shape=piece,
        in_specs=[vmem()] * chips,
        out_specs=vmem(),
        compiler_params=params(),
    )(mine, *arrived)


def over_dp(share):
    slabs = lax.axis_size("dp")
    copies = [share]
    for step in range(1, slabs):
        copies.append(lax.ppermute(share, "dp", [(i, i ^ step) for i in range(slabs)]))
    return copies


def paired_sum(values):
    while len(values) > 1:
        values = [values[i] + values[i + 1] for i in range(0, len(values), 2)]
    return values[0]


def finish_kernel(slabs, *refs):
    early_refs, late_refs = refs[:slabs], refs[slabs : 2 * slabs]
    edge_ref, down_ref, bil_ref, up_ref = refs[2 * slabs :]
    rows, model = edge_ref.shape
    basis = bil_ref.shape[0]
    _, narrow, _ = up_ref.shape
    padded = 128
    span = bil_ref.shape[1] // narrow * padded

    def total(in_refs, *part):
        return paired_sum([in_ref[part].astype(f32) for in_ref in in_refs])

    every = slice(None)
    for c in range(bil_ref.shape[1] // narrow):
        block = total(early_refs, every, slice(c * padded, (c + 1) * padded))
        bil_ref[:, c * narrow : (c + 1) * narrow] = block.T[:basis, :]
    both = total(early_refs, slice(0, rows), slice(span, span + 2 * narrow)).T
    up_ref[0] = both[:narrow, :]
    up_ref[1] = both[narrow:, :]
    edge_ref[...] = total(late_refs, every, slice(0, model))
    down_ref[...] = total(late_refs, every, slice(model, model + 2 * narrow))[:, :narrow]


def finish(early, late, basis, narrow, model, parts):
    rows = model // parts
    return pl.pallas_call(
        functools.partial(finish_kernel, len(early)),
        out_shape=(
            jax.ShapeDtypeStruct((rows, model), f32),
            jax.ShapeDtypeStruct((rows, narrow), f32),
            jax.ShapeDtypeStruct((basis, narrow * narrow // parts), f32),
            jax.ShapeDtypeStruct((2, narrow, rows), f32),
        ),
        in_specs=[vmem()] * (len(early) + len(late)),
        out_specs=(vmem(),) * 4,
        compiler_params=params(),
        name="finish",
    )(*early, *late)


def body(
    messages,
    cotangent,
    triplet_basis,
    w_edge,
    w_down,
    w_bil,
    w_up,
    trip_src,
    send_rows,
    send_count,
    rev_src,
    edge_count,
):
    _, edges, model = messages.shape
    narrow = w_down.shape[1]
    w_down = w_down.T
    slots = trip_src.shape[2]
    _, lists, capacity = send_rows.shape
    basis_count = w_bil.shape[0]
    parts = lax.axis_size("graph")
    scale = 1.0 / math.sqrt(lax.axis_size("dp") * parts * edges)
    shifts = offsets(lists)
    place = lax.axis_index("graph").reshape(1, 1)
    core, chip = place % 2, place // 2

    def exchange(blocks, sign):
        moved = []
        for which in range(lists):
            moved.append(shifted(blocks[which], "graph", sign * shifts[which]))
        return moved

    pre, hidden, pdt, red, *send_red = front(messages, w_edge, w_down, send_rows, send_count)
    recv_red = exchange(send_red, 1)
    low, high, *send_cot = pick(cotangent, send_rows, send_count, trip_src, red)
    recv_cot = exchange(send_cot, 1)
    bas = align(triplet_basis, basis_count, slots, send_cot[0])
    outer, state, wide = forward(bas, low, high, red, recv_red, w_bil)
    grad_state, up = state_grads(edge_count, state, cotangent, rev_src, recv_cot, w_up)
    keep, give = bil_shares(core, outer, grad_state, up, scale, parts)
    early = over_graph(keep, give, chip)
    home, *returned = backward(bas, grad_state, low, high, wide, capacity, lists)
    back = exchange(returned, -1)
    early = over_dp(early)
    grad_messages, keep, give = tail(
        home, back, send_rows, send_count, core, pdt, pre, hidden, messages, w_edge, w_down,
        scale, parts,
    )
    late = over_dp(over_graph(keep, give, chip))
    edge_out, down_out, bil_out, up_out = finish(early, late, basis_count, narrow, model, parts)
    return (grad_messages, edge_out, down_out, bil_out, up_out)


def solution(mesh):
    return jax.shard_map(
        body,
        mesh=mesh,
        in_specs=(
            P("dp", "graph", None),
            P("dp", "graph", None),
            P("dp", "graph", None),
            P(),
            P(),
            P(),
            P(),
            P("dp", "graph", None),
            P("dp", "graph", None),
            P("dp", "graph"),
            P("dp", "graph"),
            P("dp", "graph"),
        ),
        out_specs=(
            P("dp", "graph", None),
            P("graph", None),
            P("graph", None),
            P(None, "graph"),
            P(None, None, "graph"),
        ),
        check_vma=False,
    )
```

```python
import functools
import math

import jax
import jax.numpy as jnp
from jax import lax
from jax.experimental import pallas as pl
from jax.experimental.pallas import tpu as pltpu
from jax.sharding import PartitionSpec as P


inv_root = 0.7071067811865476
bf16 = jnp.bfloat16
f32 = jnp.float32
GROUP = 8
NN = (((1,), (0,)), ((), ()))
NT = (((1,), (1,)), ((), ()))
TN = (((0,), (0,)), ((), ()))


def mm(left, right, dims=NN):
    return lax.dot_general(left, right, dims, preferred_element_type=f32)


def silu_slope(values):
    sigma = jax.nn.sigmoid(values)
    return sigma * (1.0 + values * (1.0 - sigma))


def offsets(count):
    return [(which // 2 + 1) * (1 - 2 * (which % 2)) for which in range(count)]


def shifted(block, axis, distance):
    devices = range(lax.axis_size(axis))
    route = [((i - distance) % len(devices), i) for i in devices]
    return lax.ppermute(block, axis, route)


def iota(shape, dim):
    return lax.broadcasted_iota(jnp.int32, shape, dim)


def one_hot(index, shape, dim):
    return jnp.where(index == iota(shape, dim), 1.0, 0.0).astype(bf16)


def vmem():
    return pl.BlockSpec(memory_space=pltpu.VMEM)


def params(mib=12):
    return pltpu.CompilerParams(vmem_limit_bytes=mib * 1024 * 1024)


def cost(edges, weight):
    return pl.CostEstimate(
        flops=weight * edges * 10**6, transcendentals=0, bytes_accessed=weight * edges * 1000
    )


def send_hot(rows_ref, count_ref, which, edges):
    capacity = rows_ref.shape[2]
    rows = rows_ref[0, which : which + 1, :]
    used = iota((1, capacity), 1) < count_ref[0, which]
    return one_hot(jnp.where(used, rows, -1), (edges, capacity), 0)


def front_kernel(
    count_ref, x_ref, we_ref, wd_ref, rows_ref, pre_ref, hid_ref, pdt_ref, red_ref, *send_refs
):
    edges = x_ref.shape[1]
    step = 256
    for start in range(0, edges, step):
        pre = mm(x_ref[0, start : start + step, :], we_ref[...])
        pre_ref[start : start + step, :] = pre
        hidden = (pre * jax.nn.sigmoid(pre)).astype(bf16)
        hid_ref[start : start + step, :] = hidden
        down = mm(wd_ref[...], hidden, NT)
        pdt_ref[:, start : start + step] = down
        red_ref[:, start : start + step] = (down * jax.nn.sigmoid(down)).astype(bf16)
    for which, send_ref in enumerate(send_refs):
        hot = send_hot(rows_ref, count_ref, which, edges)
        send_ref[...] = mm(red_ref[...], hot).astype(bf16)


def smem():
    return pl.BlockSpec(memory_space=pltpu.SMEM)


def front(messages, w_edge, w_down, rows, counts):
    _, edges, model = messages.shape
    narrow = w_down.shape[0]
    _, lists, capacity = rows.shape
    return pl.pallas_call(
        front_kernel,
        out_shape=(
            jax.ShapeDtypeStruct((edges, model), f32),
            jax.ShapeDtypeStruct((edges, model), bf16),
            jax.ShapeDtypeStruct((narrow, edges), f32),
            jax.ShapeDtypeStruct((narrow, edges), bf16),
        )
        + (jax.ShapeDtypeStruct((narrow, capacity), bf16),) * lists,
        in_specs=[smem()] + [vmem()] * 4,
        out_specs=(vmem(),) * (4 + lists),
        compiler_params=params(56),
        cost_estimate=cost(edges, 3),
        name="front",
    )(counts, messages, w_edge, w_down, rows)


def pick_kernel(count_ref, cot_ref, rows_ref, trip_ref, after_ref, low_ref, high_ref, *send_refs):
    edges = cot_ref.shape[1]
    capacity = rows_ref.shape[2]
    groups, rho = low_ref.shape
    slots = rho // GROUP
    trip = trip_ref[0]
    repeat = one_hot(iota((slots, rho), 1) // GROUP, (slots, rho), 0)
    own = iota((edges, rho), 0) % GROUP == iota((edges, rho), 1) % GROUP
    gather = one_hot(iota((groups, edges), 1) // GROUP, (groups, edges), 0)

    def slot_major(values):
        spread = mm(values.astype(f32).astype(bf16), repeat)
        return mm(gather, jnp.where(own, spread, 0.0).astype(bf16))

    low_ref[...] = slot_major(jnp.bitwise_and(trip, capacity - 1))
    high_ref[...] = slot_major(jnp.right_shift(trip, capacity.bit_length() - 1)).astype(jnp.int32)
    for which, send_ref in enumerate(send_refs):
        hot = send_hot(rows_ref, count_ref, which, edges)
        send_ref[...] = mm(hot, cot_ref[0], TN).astype(bf16)


def pick(cotangent, rows, counts, trips, after):
    _, edges, model = cotangent.shape
    _, lists, capacity = rows.shape
    slot_major = (edges // GROUP, trips.shape[2] * GROUP)
    return pl.pallas_call(
        pick_kernel,
        out_shape=(
            jax.ShapeDtypeStruct(slot_major, f32),
            jax.ShapeDtypeStruct(slot_major, jnp.int32),
        )
        + (jax.ShapeDtypeStruct((capacity, model), bf16),) * lists,
        in_specs=[smem(), vmem(), vmem(), vmem(), pl.BlockSpec(memory_space=pl.ANY)],
        out_specs=(vmem(),) * (2 + lists),
        compiler_params=params(12),
        cost_estimate=cost(edges, 3),
        name="pick",
    )(counts, cotangent, rows, trips, after)


def widen_weights(wb_ref, wide):
    basis, _ = wb_ref.shape
    narrow = wide.shape[1]
    padded = wide.shape[0] // narrow
    zeros = jnp.zeros((padded - basis, narrow), bf16)
    for c in range(0, narrow, 2):
        pair = wb_ref[:, c * narrow : (c + 2) * narrow]
        wide[c * padded : (c + 1) * padded, :] = jnp.concatenate(
            [pair[:, :narrow], zeros], axis=0
        )
        wide[(c + 1) * padded : (c + 2) * padded, :] = jnp.concatenate(
            [pair[:, narrow:], zeros], axis=0
        )


def low_iota(capacity, rho):
    return iota((capacity, rho), 0).astype(f32).astype(bf16)


def low_hot(low, numbers):
    one, zero = jnp.ones((), bf16), jnp.zeros((), bf16)
    return jnp.where(low == numbers, one, zero)


def align_kernel(basis_count, sub, after_ref, basis_ref, bas_ref, slot_s):
    groups, rho, _ = slot_s.shape
    slots = rho // GROUP

    def body(index, carry):
        x = basis_ref[0, pl.ds(pl.multiple_of(index * sub, sub), sub), :].astype(f32)
        for k in range(slots):
            tile, off = divmod(k * basis_count, 128)
            if off + basis_count <= 128:
                part = x[:, tile * 128 : tile * 128 + 128]
                if off:
                    part = pltpu.roll(part, 128 - off, 1)
            else:
                part = pltpu.roll(x[:, tile * 128 : tile * 128 + 256], 256 - off, 1)[:, :128]
            for g in range(groups):
                slot_s[g, k * GROUP : (k + 1) * GROUP, :] = part[g * GROUP : (g + 1) * GROUP, :]
        for g in range(groups):
            first = pl.multiple_of((index * groups + g) * rho, rho)
            bas_ref[pl.ds(first, rho), :] = slot_s[g].astype(bf16)
        return carry

    lax.fori_loop(0, basis_ref.shape[1] // sub, body, 0)


def align(triplet_basis, basis_count, slots, after):
    _, edges, wide = triplet_basis.shape
    rho = slots * GROUP
    padded = 128
    block = 128
    sub = 64
    return pl.pallas_call(
        functools.partial(align_kernel, basis_count, sub),
        grid=(edges // block,),
        out_shape=jax.ShapeDtypeStruct((edges * slots, padded), bf16),
        in_specs=[
            pl.BlockSpec(memory_space=pl.ANY),
            pl.BlockSpec((1, block, wide), lambda i: (0, i, 0)),
        ],
        out_specs=pl.BlockSpec((block * slots, padded), lambda i: (i, 0)),
        scratch_shapes=[pltpu.VMEM((sub // GROUP, rho, padded), f32)],
        compiler_params=params(12),
        cost_estimate=cost(edges, 6),
        name="align",
    )(after, triplet_basis)


def halves(bas):
    first = iota(bas.shape, 0) % GROUP < GROUP // 2
    zero = jnp.zeros_like(bas)
    return jnp.concatenate([jnp.where(first, bas, zero), jnp.where(first, zero, bas)], axis=1)


def forward_kernel(sub, lists, bas_ref, low_ref, high_ref, red_ref, wb_ref, *rest):
    recv_refs = rest[:lists]
    outer_ref, state_ref, wide, pool, gat_s, num_s = rest[lists:]
    narrow, edges = red_ref.shape
    capacity = recv_refs[0].shape[1]
    rho = low_ref.shape[1]
    padded = bas_ref.shape[1]
    locals_ = edges // capacity

    @pl.when(pl.program_id(0) == 0)
    def _():
        for h in range(locals_):
            pool[h * narrow : (h + 1) * narrow, :] = red_ref[:, h * capacity : (h + 1) * capacity]
        for h in range(lists):
            pool[(locals_ + h) * narrow : (locals_ + h + 1) * narrow, :] = recv_refs[h][...]
        widen_weights(wb_ref, wide)
        num_s[...] = low_iota(capacity, rho)

    groups = sub // GROUP
    own = iota((GROUP, rho), 1) % GROUP == iota((GROUP, rho), 0)

    def body(index, carry):
        first = pl.multiple_of(index * sub, sub)
        first_group = pl.multiple_of(index * groups, groups)

        def gather(g):
            low = low_ref[pl.ds(first_group + g, 1), :].astype(bf16)
            high = high_ref[pl.ds(first_group + g, 1), :]
            found = mm(pool[...], low_hot(low, num_s[...]))
            gathered = jnp.zeros((narrow, rho), f32)
            for h in range(locals_ + lists):
                gathered = jnp.where(high == h, found[h * narrow : (h + 1) * narrow, :], gathered)
            gat_s[g] = gathered

        def product(g):
            spread = jnp.concatenate(
                [
                    jnp.where(own, gat_s[g, pl.ds(c, GROUP, stride=0), :], 0.0)
                    for c in range(narrow)
                ],
                axis=0,
            ).astype(bf16)
            bas = bas_ref[pl.ds(pl.multiple_of((first_group + g) * rho, rho), rho), :]
            return mm(spread, bas)

        gather(0)
        held = None
        for g in range(groups):
            if g + 1 < groups:
                gather(g + 1)
            outer = product(g)
            if g % 2 == 0:
                held = outer
                continue
            rows = pl.ds(pl.multiple_of(first + (g - 1) * GROUP, 2 * GROUP), 2 * GROUP)
            for c in range(narrow):
                part = slice(c * GROUP, (c + 1) * GROUP)
                outer_ref[rows, c * padded : (c + 1) * padded] = jnp.concatenate(
                    [held[part, :], outer[part, :]], axis=0
                ).astype(bf16)
        return carry

    lax.fori_loop(0, outer_ref.shape[0] // sub, body, 0)
    state_ref[...] = mm(outer_ref[...], wide[...]).astype(bf16)


def forward(bas, low, high, red, recv, w_bil):
    narrow, edges = red.shape
    lists = len(recv)
    capacity = recv[0].shape[1]
    rho = low.shape[1]
    padded = bas.shape[1]
    block = 256
    sub = 256
    resident = lambda *shape: pl.BlockSpec(shape, lambda i: (0,) * len(shape))
    return pl.pallas_call(
        functools.partial(forward_kernel, sub, lists),
        grid=(edges // block,),
        out_shape=(
            jax.ShapeDtypeStruct((edges, narrow * padded), bf16),
            jax.ShapeDtypeStruct((edges, narrow), bf16),
            jax.ShapeDtypeStruct((narrow * padded, narrow), bf16),
        ),
        in_specs=[
            pl.BlockSpec((block * rho // GROUP, padded), lambda i: (i, 0)),
            pl.BlockSpec((block // GROUP, rho), lambda i: (i, 0)),
            pl.BlockSpec((block // GROUP, rho), lambda i: (i, 0)),
            resident(narrow, edges),
            resident(*w_bil.shape),
        ]
        + [resident(narrow, capacity)] * lists,
        out_specs=(
            pl.BlockSpec((block, narrow * padded), lambda i: (i, 0)),
            pl.BlockSpec((block, narrow), lambda i: (i, 0)),
            resident(narrow * padded, narrow),
        ),
        scratch_shapes=[
            pltpu.VMEM((edges // capacity * narrow + lists * narrow, capacity), bf16),
            pltpu.VMEM((sub // GROUP, narrow, rho), f32),
            pltpu.VMEM((capacity, rho), bf16),
        ],
        compiler_params=params(32),
        cost_estimate=cost(edges, 29),
        name="forward",
    )(bas, low, high, red, w_bil, *recv)


def settle(core_ref, keep_ref, give_ref, pair, part, even, odd):
    is_odd = core_ref[0, 0] == 1
    keep_ref[pair, :, part] = jnp.where(is_odd, odd, even).astype(bf16)
    give_ref[pair, :, part] = jnp.where(is_odd, even, odd).astype(bf16)


def state_kernel(
    lists, count_ref, state_ref, cot_ref, rev_ref, own_ref, wu_ref, *rest
):
    recv_refs = rest[:lists]
    grad_ref, up_ref, mirror_s, cast_s = rest[lists:]
    block, _ = state_ref.shape
    edges = own_ref.shape[1]
    capacity, model = recv_refs[0].shape
    pid = pl.program_id(0)

    @pl.when(pid == 0)
    def _():
        up_ref[...] = jnp.zeros_like(up_ref)

    row = rev_ref[...].astype(f32)
    reverse = jnp.broadcast_to(row, (GROUP, block)).T[:, :1].astype(jnp.int32)
    mirror = mm(one_hot(reverse, (block, edges), 1), own_ref[0])
    for which, recv_ref in enumerate(recv_refs):
        base = edges + which * capacity
        mirror = mirror + mm(one_hot(reverse - base, (block, capacity), 1), recv_ref[...])
    mirror_s[...] = mirror
    step = 64
    for start in range(0, block, step):
        part = slice(start, start + step)
        state = state_ref[part, :]
        alive = pid * block + start + iota((step, 1), 0) < count_ref[0, 0]
        scaled = jnp.where(alive, cot_ref[0, part, :].astype(f32) * inv_root, 0.0)
        cast_s[part, :model] = (scaled * silu_slope(mm(state, wu_ref[0]))).astype(bf16)
        cast_s[part, model:] = (
            mirror_s[part, :] * inv_root * silu_slope(mm(state, wu_ref[1]))
        ).astype(bf16)
    up_ref[...] += mm(state_ref[...], cast_s[...], TN)
    back_rev = mm(cast_s[:, model:], wu_ref[1], NT).astype(bf16).astype(f32)
    grad_ref[...] = (mm(cast_s[:, :model], wu_ref[0], NT) + back_rev).astype(bf16)


def state_grads(count, state, cotangent, rev, recv_cot, w_up):
    edges, narrow = state.shape
    model = cotangent.shape[2]
    block = 256
    lists = len(recv_cot)
    resident = lambda *shape: pl.BlockSpec(shape, lambda i: (0,) * len(shape))
    return pl.pallas_call(
        functools.partial(state_kernel, lists),
        grid=(edges // block,),
        out_shape=(
            jax.ShapeDtypeStruct((edges, narrow), bf16),
            jax.ShapeDtypeStruct((narrow, 2 * model), f32),
        ),
        in_specs=[
            smem(),
            pl.BlockSpec((block, narrow), lambda i: (i, 0)),
            pl.BlockSpec((1, block, model), lambda i: (0, i, 0)),
            pl.BlockSpec((1, block), lambda i: (0, i)),
            resident(1, edges, model),
            resident(*w_up.shape),
        ]
        + [resident(*recv_cot[0].shape)] * lists,
        out_specs=(
            pl.BlockSpec((block, narrow), lambda i: (i, 0)),
            resident(narrow, 2 * model),
        ),
        scratch_shapes=[
            pltpu.VMEM((block, model), f32),
            pltpu.VMEM((block, 2 * model), bf16),
        ],
        compiler_params=params(16),
        cost_estimate=cost(edges, 7),
        name="state_grads",
    )(count, state, cotangent, rev, cotangent, w_up, *recv_cot)


def bil_kernel(scale, parts, core_ref, outer_ref, grad_ref, up_ref, keep_ref, give_ref, bil_s):
    narrow, columns = bil_s.shape
    model = up_ref.shape[1] // 2
    pid = pl.program_id(0)

    @pl.when(pid == 0)
    def _():
        bil_s[...] = jnp.zeros_like(bil_s)

    wide_step = 1024
    for start in range(0, columns, wide_step):
        bil_s[:, start : start + wide_step] += mm(
            grad_ref[...], outer_ref[:, start : start + wide_step], TN
        )

    @pl.when(pid == pl.num_programs(0) - 1)
    def _():
        span = columns // parts
        thin = model // parts
        both = jnp.concatenate([up_ref[:, :model], up_ref[:, model:]], axis=0).T
        if thin < narrow:
            spare = jnp.zeros((narrow - thin, 2 * narrow), f32)
        for pair in range(parts // 2):
            even = slice(2 * pair * span, (2 * pair + 1) * span)
            odd = slice((2 * pair + 1) * span, (2 * pair + 2) * span)
            settle(core_ref, keep_ref, give_ref, pair, slice(0, span),
                   bil_s[:, even] * scale, bil_s[:, odd] * scale)
            sides = []
            for dest in (2 * pair, 2 * pair + 1):
                piece = both[dest * thin : (dest + 1) * thin, :] * scale
                if thin < narrow:
                    piece = jnp.concatenate([piece, spare], axis=0)
                sides.append(piece)
            settle(core_ref, keep_ref, give_ref, pair, slice(span, span + 2 * narrow), *sides)


def bil_shares(core, outer, grad_state, up, scale, parts):
    edges, narrow = grad_state.shape
    columns = outer.shape[1]
    block = 256
    share = (parts // 2, narrow, columns // parts + 2 * narrow)
    resident = lambda *shape: pl.BlockSpec(shape, lambda i: (0,) * len(shape))
    return pl.pallas_call(
        functools.partial(bil_kernel, scale, parts),
        grid=(edges // block,),
        out_shape=(jax.ShapeDtypeStruct(share, bf16),) * 2,
        in_specs=[
            smem(),
            pl.BlockSpec((block, columns), lambda i: (i, 0)),
            pl.BlockSpec((block, narrow), lambda i: (i, 0)),
            resident(*up.shape),
        ],
        out_specs=(resident(*share),) * 2,
        scratch_shapes=[pltpu.VMEM((narrow, columns), f32)],
        compiler_params=params(20),
        cost_estimate=cost(edges, 4),
        name="bil_shares",
    )(core, outer, grad_state, up)


def own_rows(mixed, narrow):
    rho = mixed.shape[1]
    half = GROUP // 2
    value = mixed.reshape(narrow // GROUP, half, GROUP, rho)
    shape = (1, 1, GROUP, rho)
    row, lane = iota(shape, 2), iota(shape, 3)
    step = half // 2
    while step:
        low, high = value[:, :step], value[:, step:]
        upper = jnp.bitwise_and(row, step) > 0
        kept = jnp.bitwise_and(row, step) == jnp.bitwise_and(lane, step)
        straight = jnp.where(upper, high, low)
        other = jnp.where(upper, low, high)
        moved = jnp.where(
            upper, pltpu.roll(other, step, 2), pltpu.roll(other, GROUP - step, 2)
        )
        value = jnp.where(kept, straight, moved)
        step //= 2
    return value.reshape(narrow, rho)


def backward_kernel(sub, lists, bas_ref, grad_ref, low_ref, high_ref, wide, home_ref, *rest):
    back_refs = rest[:lists]
    pool_s, turn_s, cast_s, hot_s, num_s = rest[lists:]
    block, narrow = grad_ref.shape
    padded = bas_ref.shape[1]
    rho = low_ref.shape[1]
    rows, capacity = pool_s.shape
    pid = pl.program_id(0)

    @pl.when(pid == 0)
    def _():
        pool_s[...] = jnp.zeros_like(pool_s)
        num_s[...] = low_iota(capacity, rho)

    grad_state = grad_ref[...]
    half = GROUP // 2
    height = narrow * half
    top = iota((GROUP, 1), 0) < half

    def spread(tile, carry):
        start = pl.multiple_of(tile * GROUP * padded, GROUP * padded)
        grad = mm(grad_state, wide[pl.ds(start, GROUP * padded), :], NT)
        for g in range(block // GROUP):
            part = slice(g * GROUP, (g + 1) * GROUP)
            sides = []
            for c in range(half):
                near = grad[part, c * padded : (c + 1) * padded]
                far = grad[part, (c + half) * padded : (c + half + 1) * padded]
                left = jnp.where(top, near, pltpu.roll(far, half, 0))
                right = jnp.where(top, pltpu.roll(near, half, 0), far)
                sides.append(jnp.concatenate([left, right], axis=1))
            at = pl.multiple_of(g * height + tile * GROUP * half, GROUP * half)
            turn_s[pl.ds(at, GROUP * half), :] = jnp.concatenate(sides, axis=0).astype(bf16)
        return carry

    lax.fori_loop(0, narrow // GROUP, spread, 0, unroll=4)
    groups = sub // GROUP

    def body(index, carry):
        first_group = pl.multiple_of(index * groups, groups)

        def mix(g):
            here = first_group + g
            bas = bas_ref[pl.ds(pl.multiple_of(here * rho, rho), rho), :]
            grads = turn_s[pl.ds(pl.multiple_of(here * height, height), height), :]
            return mm(grads, halves(bas), NT)

        def cast(g, mixed):
            trip_grad = own_rows(mixed, narrow).astype(bf16)
            low = low_ref[pl.ds(first_group + g, 1), :].astype(bf16)
            high = high_ref[pl.ds(first_group + g, 1), :]
            part = slice(g * rho, (g + 1) * rho)
            hot_s[:, part] = low_hot(low, num_s[...])
            zero = jnp.zeros_like(trip_grad)
            wide_high = jnp.broadcast_to(high.astype(f32).astype(bf16), trip_grad.shape)
            for h in range(rows // narrow):
                cast_s[h * narrow : (h + 1) * narrow, part] = jnp.where(
                    wide_high == jnp.asarray(h, bf16), trip_grad, zero
                )

        ready = mix(0)
        for g in range(groups):
            mixed = ready
            if g + 1 < groups:
                ready = mix(g + 1)
            cast(g, mixed)
        pool_s[...] += mm(cast_s[...], hot_s[...], NT)
        return carry

    lax.fori_loop(0, block // sub, body, 0)

    @pl.when(pid == pl.num_programs(0) - 1)
    def _():
        home = home_ref.shape[0]
        home_ref[...] = pool_s[:home, :]
        for which, back_ref in enumerate(back_refs):
            first = home + which * narrow
            back_ref[...] = pool_s[first : first + narrow, :].astype(bf16)


def backward(bas, grad_state, low, high, wide, capacity, lists):
    edges, narrow = grad_state.shape
    rho = low.shape[1]
    padded = bas.shape[1]
    block = 256
    sub = 256
    home = edges // capacity * narrow
    rows = home + lists * narrow
    resident = lambda *shape: pl.BlockSpec(shape, lambda i: (0,) * len(shape))
    return pl.pallas_call(
        functools.partial(backward_kernel, sub, lists),
        grid=(edges // block,),
        out_shape=(jax.ShapeDtypeStruct((home, capacity), f32),)
        + (jax.ShapeDtypeStruct((narrow, capacity), bf16),) * lists,
        in_specs=[
            pl.BlockSpec((block * rho // GROUP, padded), lambda i: (i, 0)),
            pl.BlockSpec((block, narrow), lambda i: (i, 0)),
            pl.BlockSpec((block // GROUP, rho), lambda i: (i, 0)),
            pl.BlockSpec((block // GROUP, rho), lambda i: (i, 0)),
            resident(*wide.shape),
        ],
        out_specs=(resident(home, capacity),) + (resident(narrow, capacity),) * lists,
        scratch_shapes=[
            pltpu.VMEM((rows, capacity), f32),
            pltpu.VMEM((block * narrow // 2, 2 * padded), bf16),
            pltpu.VMEM((rows, sub // GROUP * rho), bf16),
            pltpu.VMEM((capacity, sub // GROUP * rho), bf16),
            pltpu.VMEM((capacity, rho), bf16),
        ],
        compiler_params=params(32),
        cost_estimate=cost(edges, 32),
        name="backward",
    )(bas, grad_state, low, high, wide)


def tail_kernel(
    scale, parts, lists,
    count_ref, core_ref, pool_ref, rows_ref, pdt_ref, pre_ref, hid_ref, x_ref, we_ref, wd_ref, *rest
):
    back_refs = rest[:lists]
    out_ref, keep_ref, give_ref, grad_s = rest[lists:]
    narrow, edges = pdt_ref.shape
    capacity = back_refs[0].shape[1]
    model = pre_ref.shape[1]
    grad = jnp.concatenate(
        [pool_ref[h * narrow : (h + 1) * narrow, :] for h in range(edges // capacity)], axis=1
    )
    for which, back_ref in enumerate(back_refs):
        grad = grad + mm(back_ref[...], send_hot(rows_ref, count_ref, which, edges), NT)
    grad_down = (grad * silu_slope(pdt_ref[...])).astype(bf16)
    step = 256
    for start in range(0, edges, step):
        part = slice(start, start + step)
        grad_hidden = mm(grad_down[:, part], wd_ref[...], TN)
        grad_edge = (grad_hidden * silu_slope(pre_ref[part, :])).astype(bf16)
        grad_s[part, :] = grad_edge
        out_ref[0, part, :] = mm(grad_edge, we_ref[...], NT).astype(bf16)
    down = lax.dot_general(
        hid_ref[...], grad_down, (((0,), (1,)), ((), ())), preferred_element_type=f32
    )
    down = jnp.concatenate([down, jnp.zeros_like(down)], axis=1)
    span = model // parts
    for start in range(0, model, step):
        edge = mm(x_ref[0, :, start : start + step], grad_s[...], TN)
        both = jnp.concatenate([edge, down[start : start + step, :]], axis=1) * scale
        for first in range(0, step, 2 * span):
            settle(
                core_ref, keep_ref, give_ref, (start + first) // (2 * span), slice(None),
                both[first : first + span, :], both[first + span : first + 2 * span, :],
            )


def tail(pool, back, rows, counts, core, pdt, pre, hidden, messages, w_edge, w_down, scale, parts):
    _, edges, model = messages.shape
    narrow = w_down.shape[0]
    share = jax.ShapeDtypeStruct((parts // 2, model // parts, model + 2 * narrow), bf16)
    return pl.pallas_call(
        functools.partial(tail_kernel, scale, parts, len(back)),
        out_shape=(
            jax.ShapeDtypeStruct((1, edges, model), bf16),
            share,
            share,
        ),
        in_specs=[smem(), smem()] + [vmem()] * (8 + len(back)),
        out_specs=(vmem(),) * 3,
        scratch_shapes=[pltpu.VMEM((edges, model), bf16)],
        compiler_params=params(),
        cost_estimate=cost(edges, 4),
        name="tail",
    )(counts, core, pool, rows, pdt, pre, hidden, messages, w_edge, w_down, *back)


def add_pair_kernel(chip_ref, keep_ref, got_ref, mine_ref, *out_refs):
    chips = keep_ref.shape[0]
    chip = chip_ref[0, 0]
    for step, out_ref in enumerate((mine_ref,) + out_refs):
        at = lax.rem(chip + step, chips)
        out_ref[...] = (keep_ref[at].astype(f32) + got_ref[at].astype(f32)).astype(bf16)


def add_kernel(*refs):
    *in_refs, out_ref = refs
    total = in_refs[0][...].astype(f32)
    for in_ref in in_refs[1:]:
        total = total + in_ref[...].astype(f32)
    out_ref[...] = total.astype(bf16)


def over_graph(keep, give, chip):
    chips, height, wide = keep.shape
    devices = 2 * chips
    piece = jax.ShapeDtypeStruct((height, wide), bf16)
    got = lax.ppermute(give, "graph", [(i, i ^ 1) for i in range(devices)])
    mine, *sends = pl.pallas_call(
        add_pair_kernel,
        out_shape=(piece,) * chips,
        in_specs=[smem(), vmem(), vmem()],
        out_specs=(vmem(),) * chips,
        compiler_params=params(),
    )(chip, keep, got)
    arrived = []
    for step, send in enumerate(sends):
        route = [(i, (i + 2 * (step + 1)) % devices) for i in range(devices)]
        arrived.append(lax.ppermute(send, "graph", route))
    return pl.pallas_call(
        add_kernel,
        out_shape=piece,
        in_specs=[vmem()] * chips,
        out_specs=vmem(),
        compiler_params=params(),
    )(mine, *arrived)


def over_dp(share):
    slabs = lax.axis_size("dp")
    copies = [share]
    for step in range(1, slabs):
        copies.append(lax.ppermute(share, "dp", [(i, i ^ step) for i in range(slabs)]))
    return copies


def paired_sum(values):
    while len(values) > 1:
        values = [values[i] + values[i + 1] for i in range(0, len(values), 2)]
    return values[0]


def finish_kernel(slabs, *refs):
    early_refs, late_refs = refs[:slabs], refs[slabs : 2 * slabs]
    edge_ref, down_ref, bil_ref, up_ref = refs[2 * slabs :]
    rows, model = edge_ref.shape
    basis = bil_ref.shape[0]
    _, narrow, _ = up_ref.shape
    padded = 128
    span = bil_ref.shape[1] // narrow * padded

    def total(in_refs, *part):
        return paired_sum([in_ref[part].astype(f32) for in_ref in in_refs])

    every = slice(None)
    for c in range(bil_ref.shape[1] // narrow):
        block = total(early_refs, every, slice(c * padded, (c + 1) * padded))
        bil_ref[:, c * narrow : (c + 1) * narrow] = block.T[:basis, :]
    both = total(early_refs, slice(0, rows), slice(span, span + 2 * narrow)).T
    up_ref[0] = both[:narrow, :]
    up_ref[1] = both[narrow:, :]
    edge_ref[...] = total(late_refs, every, slice(0, model))
    down_ref[...] = total(late_refs, every, slice(model, model + 2 * narrow))[:, :narrow]


def finish(early, late, basis, narrow, model, parts):
    rows = model // parts
    return pl.pallas_call(
        functools.partial(finish_kernel, len(early)),
        out_shape=(
            jax.ShapeDtypeStruct((rows, model), f32),
            jax.ShapeDtypeStruct((rows, narrow), f32),
            jax.ShapeDtypeStruct((basis, narrow * narrow // parts), f32),
            jax.ShapeDtypeStruct((2, narrow, rows), f32),
        ),
        in_specs=[vmem()] * (len(early) + len(late)),
        out_specs=(vmem(),) * 4,
        compiler_params=params(),
        name="finish",
    )(*early, *late)


def body(
    messages,
    cotangent,
    triplet_basis,
    w_edge,
    w_down,
    w_bil,
    w_up,
    trip_src,
    send_rows,
    send_count,
    rev_src,
    edge_count,
):
    _, edges, model = messages.shape
    narrow = w_down.shape[1]
    w_down = w_down.T
    slots = trip_src.shape[2]
    _, lists, capacity = send_rows.shape
    basis_count = w_bil.shape[0]
    parts = lax.axis_size("graph")
    scale = 1.0 / math.sqrt(lax.axis_size("dp") * parts * edges)
    shifts = offsets(lists)
    place = lax.axis_index("graph").reshape(1, 1)
    core, chip = place % 2, place // 2

    def exchange(blocks, sign):
        moved = []
        for which in range(lists):
            moved.append(shifted(blocks[which], "graph", sign * shifts[which]))
        return moved

    pre, hidden, pdt, red, *send_red = front(messages, w_edge, w_down, send_rows, send_count)
    recv_red = exchange(send_red, 1)
    low, high, *send_cot = pick(cotangent, send_rows, send_count, trip_src, red)
    recv_cot = exchange(send_cot, 1)
    bas = align(triplet_basis, basis_count, slots, send_cot[0])
    outer, state, wide = forward(bas, low, high, red, recv_red, w_bil)
    grad_state, up = state_grads(edge_count, state, cotangent, rev_src, recv_cot, w_up)
    keep, give = bil_shares(core, outer, grad_state, up, scale, parts)
    early = over_graph(keep, give, chip)
    home, *returned = backward(bas, grad_state, low, high, wide, capacity, lists)
    back = exchange(returned, -1)
    early = over_dp(early)
    grad_messages, keep, give = tail(
        home, back, send_rows, send_count, core, pdt, pre, hidden, messages, w_edge, w_down,
        scale, parts,
    )
    late = over_dp(over_graph(keep, give, chip))
    edge_out, down_out, bil_out, up_out = finish(early, late, basis_count, narrow, model, parts)
    return (grad_messages, edge_out, down_out, bil_out, up_out)


def solution(mesh):
    return jax.shard_map(
        body,
        mesh=mesh,
        in_specs=(
            P("dp", "graph", None),
            P("dp", "graph", None),
            P("dp", "graph", None),
            P(),
            P(),
            P(),
            P(),
            P("dp", "graph", None),
            P("dp", "graph", None),
            P("dp", "graph"),
            P("dp", "graph"),
            P("dp", "graph"),
        ),
        out_specs=(
            P("dp", "graph", None),
            P("graph", None),
            P("graph", None),
            P(None, "graph"),
            P(None, None, "graph"),
        ),
        check_vma=False,
    )
```
